32 devices in a mesh: cross: 4 (over y, x), island: 8 (over z, core).
Axes of the slice: x: 2, y: 2, z: 4, core: 2. Of those that a mesh axis runs over, the one named last changes fastest.
Arguments:
- tokens: bfloat16 [16384, 768], P(('cross', 'island')), may hold values from -6 to 6
- cotangent: bfloat16 [16384, 768], P(('cross', 'island')), may hold values from -6 to 6
- gate: float32 [16384], P(('cross', 'island')), may hold values from 0.2 to 1
- slot: int32 [16384], P(('cross', 'island')), may hold values from -1 to 127, as said below
- w_in: bfloat16 [64, 768, 3072], P(('cross', 'island')), may hold values from -0.21875 to 0.21875
- w_out: bfloat16 [64, 3072, 768], P(('cross', 'island')), may hold values from -0.109375 to 0.109375
Outputs:
- token_grad: bfloat16 [16384, 768], P(('cross', 'island'))
The draws below stay inside these ranges and needn't reach their ends.
Inputs may be any that keep to these rules, and one draw needn't show every extreme that they name: Within the tokens of one device the non-negative slots are distinct; slot // 2 is the token's expert and its slots are filled from 0 upward in token order; tokens beyond an expert's 2 slots are -1. Expert indices run over devices in mesh order, 2 a device.
All inputs are finite; a program needn't handle non-finite values.
Results may differ from the reference program's by a relative error of at most 0.0057.
Values may be sent and summed in bfloat16 or wider, within the bound.
No kernel may reach another device: no remote copies, remote signals or barrier semaphores. Data moves between devices by JAX's collectives and lax.ppermute only.
A program may use at most 128 MiB of HBM per device.

```python
import jax
import jax.numpy as jnp
from jax import lax

D = 768
FF = 3072
CAP = 2
TOK_DEV = 512
EXPERTS = 64
TOKENS = 16384
N_CROSS = 4
N_ISLAND = 8


def draw_slot(key, part):
    devices = N_CROSS * N_ISLAND
    key_expert = jax.random.fold_in(key, 11)
    key_hot = jax.random.fold_in(key, 23)
    chosen = jax.random.randint(key_expert, (devices, TOK_DEV), 0, EXPERTS)
    hot = jax.random.randint(key_hot, (), 0, EXPERTS)
    position = jnp.arange(TOK_DEV)[None, :]
    chosen = jnp.where(position < CAP, hot, chosen)
    first_block = jnp.arange(devices)[:, None] == 0
    chosen = jnp.where(first_block & (position >= TOK_DEV - CAP), EXPERTS - 1, chosen)
    onehot = (chosen[:, :, None] == jnp.arange(EXPERTS)[None, None, :]).astype(jnp.int32)
    earlier = jnp.cumsum(onehot, axis=1) - onehot
    rank = jnp.sum(earlier * onehot, axis=2)
    slots = jnp.where(rank < CAP, chosen * CAP + rank, -1)
    return slots.reshape(devices * TOK_DEV).astype(jnp.int32)


def block_scale(rng, dims, shards, low, top_value):
    def one(dim, blocks):
        steps = jax.random.uniform(jax.random.fold_in(jax.random.fold_in(rng, 6), dim), (blocks,), jnp.float32, low / len(shards), top_value / len(shards))
        return jnp.repeat(jnp.exp(steps), dims[dim] // blocks).reshape((-1,) + (1,) * (len(dims) - dim - 1))

    gain = one(*shards[0])
    for cut in shards[1:]:
        gain = gain * one(*cut)
    return gain


def gaussian(key, extent, scale, bound, pieces=(), kind=jnp.bfloat16):
    loudness = block_scale(key, extent, pieces, -0.22, 0.18) if pieces else 1.0
    drawn = jax.random.normal(key, extent, jnp.float32) * scale * loudness
    return jnp.minimum(jnp.maximum(drawn, -bound), bound).astype(kind)


def setup_inputs(seed: int = 0) -> dict:
    key_list = jax.random.split(jax.random.key(seed), 7)
    return {
        "tokens": gaussian(key_list[0], (TOKENS, D), 1.0, 6.0, ((0, 32),)),
        "cotangent": gaussian(key_list[1], (TOKENS, D), 1.0, 6.0, ((0, 32),)),
        "gate": jnp.clip(0.2 + 0.8 * jax.random.uniform(key_list[2], (TOKENS,), jnp.float32) ** block_scale(key_list[2], (TOKENS,), ((0, 32),), -0.2, 0.2), 0.2, 1.0),
        "slot": draw_slot(jax.random.fold_in(key_list[6], 71), 0),
        "w_in": gaussian(key_list[4], (EXPERTS, D, FF), D ** -0.5, 0.21875, ((0, 32),)),
        "w_out": gaussian(key_list[5], (EXPERTS, FF, D), FF ** -0.5, 0.109375, ((0, 32),)),
    }


def ramp(pre):
    return jnp.clip(0.5 + 10.0 * pre, 0.0, 1.0)


def reference(tokens, cotangent, gate, slot, w_in, w_out):
    devices = N_CROSS * N_ISLAND
    experts = EXPERTS
    scaled = (gate[:, None] * cotangent.astype(jnp.float32)).astype(jnp.bfloat16)
    blocks_x = tokens.reshape(devices, TOK_DEV, D)
    blocks_d = scaled.reshape(devices, TOK_DEV, D)
    slots = slot.reshape(devices, TOK_DEV)
    target = jnp.where(slots < 0, experts * CAP, slots).astype(jnp.int32)

    def place(rows, where_to):
        return jnp.zeros((experts * CAP, D), rows.dtype).at[where_to].set(rows, mode="drop")

    def to_experts(buffer):
        buffer = jax.vmap(place)(buffer, target)
        return buffer.reshape(devices, experts, CAP, D).transpose(1, 0, 2, 3).reshape(experts, devices * CAP, D)

    sent_x = to_experts(blocks_x)
    sent_d = to_experts(blocks_d)

    def expert(items):
        rows_x, rows_d, first, second = items
        pre = jnp.dot(rows_x, first, preferred_element_type=jnp.float32)
        back = jnp.dot(rows_d, second.T, preferred_element_type=jnp.float32)
        hidden_grad = (back * ramp(pre)).astype(jnp.bfloat16)
        return jnp.dot(hidden_grad, first.T, preferred_element_type=jnp.float32).astype(jnp.bfloat16)

    result = lax.map(expert, (sent_x, sent_d, w_in, w_out))
    result = result.reshape(experts, devices, CAP, D).transpose(1, 0, 2, 3).reshape(devices, experts * CAP, D)
    safe = jnp.where(slots < 0, 0, slots).astype(jnp.int32)
    picked = jnp.take_along_axis(result, safe[:, :, None], axis=1)
    picked = jnp.where(slots[:, :, None] >= 0, picked, jnp.zeros_like(picked))
    return picked.reshape(TOKENS, D).astype(jnp.bfloat16)
```

```python
import functools

import jax
import jax.numpy as jnp
from jax import lax
from jax.experimental import pallas as pl
from jax.experimental.pallas import tpu as pltpu
from jax.sharding import PartitionSpec as P

CAP = 2
AXES = ("cross", "island")
MIB = 1 << 20


def ramp(pre):
    return jnp.clip(0.5 + 10.0 * pre, 0.0, 1.0)


def split(value, size):
    if size & (size - 1) == 0:
        return value >> (size.bit_length() - 1), value & (size - 1)
    return lax.div(value, size), lax.rem(value, size)


def one_hot(mask):
    return jnp.where(mask, 1.0, 0.0).astype(jnp.bfloat16)


def send_kernel(per_dev, slot_ref, gate_ref, tokens_ref, cotangent_ref, out_ref):
    shape = (out_ref.shape[0], slot_ref.shape[1])
    device, within = split(lax.broadcasted_iota(jnp.int32, shape, 0), 2 * per_dev)
    kind, place = split(within, per_dev)
    match = slot_ref[...] == device * per_dev + place
    is_d = kind == 1
    rows = jnp.dot(
        one_hot(match & ~is_d), tokens_ref[...], preferred_element_type=jnp.float32
    ) + jnp.dot(
        one_hot(match & is_d), cotangent_ref[...], preferred_element_type=jnp.float32
    )
    gate = jnp.sum(jnp.where(match, gate_ref[...], 0.0), axis=1, keepdims=True)
    out_ref[...] = (rows * jnp.where(is_d[:, :1], gate, 1.0)).astype(out_ref.dtype)


def expert_kernel(experts, chunk, recv_ref, w_in_ref, w_out_ref, out_ref):
    per_dev = experts * CAP
    total = recv_ref.shape[0]
    devices = total // (2 * per_dev)
    rows = devices * CAP
    width = recv_ref.shape[1]
    hidden = w_in_ref.shape[2]
    to = lax.broadcasted_iota(jnp.int32, (total, total), 0)
    group, member = split(to, rows)
    device, cap = split(member, CAP)
    source = device * (2 * per_dev) + group * CAP + cap
    pick = one_hot(lax.broadcasted_iota(jnp.int32, (total, total), 1) == source)
    sorted_rows = jnp.dot(
        pick, recv_ref[...], preferred_element_type=jnp.float32
    ).astype(jnp.bfloat16)
    parts = []
    for e in range(experts):
        x = sorted_rows[e * rows : (e + 1) * rows]
        d = sorted_rows[(experts + e) * rows : (experts + e + 1) * rows]
        total_grad = jnp.zeros((rows, width), jnp.float32)
        for f in range(0, hidden, chunk):
            first = w_in_ref[e, :, f : f + chunk]
            second = w_out_ref[e, f : f + chunk, :]
            pre = jnp.dot(x, first, preferred_element_type=jnp.float32)
            back = lax.dot_general(
                d, second, (((1,), (1,)), ((), ())), preferred_element_type=jnp.float32
            )
            hidden_grad = (back * ramp(pre)).astype(jnp.bfloat16)
            total_grad += lax.dot_general(
                hidden_grad,
                first,
                (((1,), (1,)), ((), ())),
                preferred_element_type=jnp.float32,
            )
        parts.append(total_grad.astype(jnp.bfloat16))
    grads = jnp.concatenate(parts, axis=0)
    half = width // 2
    shape = (total, experts * rows)
    device, within = split(lax.broadcasted_iota(jnp.int32, shape, 0), 2 * per_dev)
    side, place = split(within, per_dev)
    expert, cap = split(place, CAP)
    match = lax.broadcasted_iota(jnp.int32, shape, 1) == (
        expert * rows + device * CAP + cap
    )
    out_ref[...] = (
        jnp.dot(
            one_hot(match & (side == 0)),
            grads[:, :half],
            preferred_element_type=jnp.float32,
        )
        + jnp.dot(
            one_hot(match & (side == 1)),
            grads[:, half:],
            preferred_element_type=jnp.float32,
        )
    ).astype(out_ref.dtype)


def token_kernel(per_dev, slot_ref, rows_ref, out_ref):
    shape = (rows_ref.shape[0], slot_ref.shape[1])
    device, within = split(lax.broadcasted_iota(jnp.int32, shape, 0), 2 * per_dev)
    side, place = split(within, per_dev)
    match = slot_ref[...] == device * per_dev + place
    half = rows_ref.shape[1]
    for k in range(2):
        out_ref[:, k * half : (k + 1) * half] = lax.dot_general(
            one_hot(match & (side == k)),
            rows_ref[...],
            (((0,), (0,)), ((), ())),
            preferred_element_type=jnp.float32,
        ).astype(out_ref.dtype)


VMEM = pl.BlockSpec(memory_space=pltpu.VMEM)


def per_device(tokens, cotangent, gate, slot, w_in, w_out):
    devices = lax.axis_size("cross") * lax.axis_size("island")
    experts, width, hidden = w_in.shape
    per_dev = experts * CAP
    total = devices * per_dev
    slot_row = slot[None, :]
    send = pl.pallas_call(
        functools.partial(send_kernel, per_dev),
        out_shape=jax.ShapeDtypeStruct((2 * total, width), jnp.bfloat16),
        in_specs=[VMEM] * 4,
        out_specs=VMEM,
        compiler_params=pltpu.CompilerParams(vmem_limit_bytes=16 * MIB),
        name="send",
    )(slot_row, gate[None, :], tokens, cotangent)
    recv = lax.all_to_all(
        send.reshape(devices, 2 * per_dev, width), AXES, 0, 0, tiled=True
    )
    result = pl.pallas_call(
        functools.partial(expert_kernel, experts, 512),
        out_shape=jax.ShapeDtypeStruct((2 * total, width // 2), jnp.bfloat16),
        in_specs=[VMEM] * 3,
        out_specs=VMEM,
        compiler_params=pltpu.CompilerParams(vmem_limit_bytes=32 * MIB),
        name="expert",
    )(recv.reshape(2 * total, width), w_in, w_out)
    arrived = lax.all_to_all(
        result.reshape(devices, 2 * per_dev, width // 2), AXES, 0, 0, tiled=True
    )
    return pl.pallas_call(
        functools.partial(token_kernel, per_dev),
        out_shape=jax.ShapeDtypeStruct(tokens.shape, jnp.bfloat16),
        in_specs=[VMEM] * 2,
        out_specs=VMEM,
        compiler_params=pltpu.CompilerParams(vmem_limit_bytes=16 * MIB),
        name="token",
    )(slot_row, arrived.reshape(2 * total, width // 2))


def solution(mesh):
    token_spec = P(AXES, None)
    weight_spec = P(AXES, None, None)
    return jax.shard_map(
        per_device,
        mesh=mesh,
        in_specs=(token_spec, token_spec, P(AXES), P(AXES), weight_spec, weight_spec),
        out_specs=token_spec,
        check_vma=False,
    )
```

```python
import functools

import jax
import jax.numpy as jnp
from jax import lax
from jax.experimental import pallas as pl
from jax.experimental.pallas import tpu as pltpu
from jax.sharding import PartitionSpec as P

CAP = 2
AXES = ("cross", "island")
MIB = 1 << 20


def ramp(pre):
    return jnp.clip(0.5 + 10.0 * pre, 0.0, 1.0)


def split(value, size):
    if size & (size - 1) == 0:
        return value >> (size.bit_length() - 1), value & (size - 1)
    return lax.div(value, size), lax.rem(value, size)


def one_hot(mask):
    return jnp.where(mask, 1.0, 0.0).astype(jnp.bfloat16)


def start_kernel(out_ref):
    out_ref[...] = jnp.zeros_like(out_ref)


def send_kernel(
    per_dev, slot_ref, gate_ref, tokens_ref, cotangent_ref, started, out_ref
):
    del started
    shape = (out_ref.shape[0], slot_ref.shape[1])
    device, within = split(lax.broadcasted_iota(jnp.int32, shape, 0), 2 * per_dev)
    kind, place = split(within, per_dev)
    match = slot_ref[...] == device * per_dev + place
    is_d = kind == 1
    rows = jnp.dot(
        one_hot(match & ~is_d), tokens_ref[...], preferred_element_type=jnp.float32
    ) + jnp.dot(
        one_hot(match & is_d), cotangent_ref[...], preferred_element_type=jnp.float32
    )
    gate = jnp.sum(jnp.where(match, gate_ref[...], 0.0), axis=1, keepdims=True)
    out_ref[...] = (rows * jnp.where(is_d[:, :1], gate, 1.0)).astype(out_ref.dtype)


def expert_kernel(experts, chunk, recv_ref, w_in_ref, w_out_ref, out_ref):
    per_dev = experts * CAP
    total = recv_ref.shape[0]
    devices = total // (2 * per_dev)
    rows = devices * CAP
    width = recv_ref.shape[1]
    hidden = w_in_ref.shape[2]
    to = lax.broadcasted_iota(jnp.int32, (total, total), 0)
    group, member = split(to, rows)
    device, cap = split(member, CAP)
    source = device * (2 * per_dev) + group * CAP + cap
    pick = one_hot(lax.broadcasted_iota(jnp.int32, (total, total), 1) == source)
    sorted_rows = jnp.dot(
        pick, recv_ref[...], preferred_element_type=jnp.float32
    ).astype(jnp.bfloat16)
    parts = []
    for e in range(experts):
        x = sorted_rows[e * rows : (e + 1) * rows]
        d = sorted_rows[(experts + e) * rows : (experts + e + 1) * rows]
        total_grad = jnp.zeros((rows, width), jnp.float32)
        for f in range(0, hidden, chunk):
            first = w_in_ref[e, :, f : f + chunk]
            second = w_out_ref[e, f : f + chunk, :]
            pre = jnp.dot(x, first, preferred_element_type=jnp.float32)
            back = lax.dot_general(
                d, second, (((1,), (1,)), ((), ())), preferred_element_type=jnp.float32
            )
            hidden_grad = (back * ramp(pre)).astype(jnp.bfloat16)
            total_grad += lax.dot_general(
                hidden_grad,
                first,
                (((1,), (1,)), ((), ())),
                preferred_element_type=jnp.float32,
            )
        parts.append(total_grad.astype(jnp.bfloat16))
    grads = jnp.concatenate(parts, axis=0)
    half = width // 2
    shape = (total, experts * rows)
    device, within = split(lax.broadcasted_iota(jnp.int32, shape, 0), 2 * per_dev)
    side, place = split(within, per_dev)
    expert, cap = split(place, CAP)
    match = lax.broadcasted_iota(jnp.int32, shape, 1) == (
        expert * rows + device * CAP + cap
    )
    out_ref[...] = (
        jnp.dot(
            one_hot(match & (side == 0)),
            grads[:, :half],
            preferred_element_type=jnp.float32,
        )
        + jnp.dot(
            one_hot(match & (side == 1)),
            grads[:, half:],
            preferred_element_type=jnp.float32,
        )
    ).astype(out_ref.dtype)


def token_kernel(per_dev, slot_ref, rows_ref, out_ref):
    shape = (rows_ref.shape[0], slot_ref.shape[1])
    device, within = split(lax.broadcasted_iota(jnp.int32, shape, 0), 2 * per_dev)
    side, place = split(within, per_dev)
    match = slot_ref[...] == device * per_dev + place
    half = rows_ref.shape[1]
    for k in range(2):
        out_ref[:, k * half : (k + 1) * half] = lax.dot_general(
            one_hot(match & (side == k)),
            rows_ref[...],
            (((0,), (0,)), ((), ())),
            preferred_element_type=jnp.float32,
        ).astype(out_ref.dtype)


VMEM = pl.BlockSpec(memory_space=pltpu.VMEM)
LONG = pl.CostEstimate(flops=20_000_000_000, transcendentals=0, bytes_accessed=0)


def per_device(tokens, cotangent, gate, slot, w_in, w_out):
    devices = lax.axis_size("cross") * lax.axis_size("island")
    experts, width, hidden = w_in.shape
    per_dev = experts * CAP
    total = devices * per_dev
    slot_row = slot[None, :]
    started = pl.pallas_call(
        start_kernel,
        out_shape=jax.ShapeDtypeStruct((8, 128), jnp.float32),
        out_specs=VMEM,
        compiler_params=pltpu.CompilerParams(vmem_limit_bytes=MIB),
        cost_estimate=LONG,
        name="start",
    )()
    send = pl.pallas_call(
        functools.partial(send_kernel, per_dev),
        out_shape=jax.ShapeDtypeStruct((2 * total, width), jnp.bfloat16),
        in_specs=[VMEM] * 4 + [pl.BlockSpec(memory_space=pl.ANY)],
        out_specs=VMEM,
        compiler_params=pltpu.CompilerParams(vmem_limit_bytes=16 * MIB),
        cost_estimate=LONG,
        name="send",
    )(slot_row, gate[None, :], tokens, cotangent, started)
    recv = lax.all_to_all(
        send.reshape(devices, 2 * per_dev, width), AXES, 0, 0, tiled=True
    )
    result = pl.pallas_call(
        functools.partial(expert_kernel, experts, 512),
        out_shape=jax.ShapeDtypeStruct((2 * total, width // 2), jnp.bfloat16),
        in_specs=[VMEM] * 3,
        out_specs=VMEM,
        compiler_params=pltpu.CompilerParams(vmem_limit_bytes=32 * MIB),
        name="expert",
    )(recv.reshape(2 * total, width), w_in, w_out)
    arrived = lax.all_to_all(
        result.reshape(devices, 2 * per_dev, width // 2), AXES, 0, 0, tiled=True
    )
    return pl.pallas_call(
        functools.partial(token_kernel, per_dev),
        out_shape=jax.ShapeDtypeStruct(tokens.shape, jnp.bfloat16),
        in_specs=[VMEM] * 2,
        out_specs=VMEM,
        compiler_params=pltpu.CompilerParams(vmem_limit_bytes=16 * MIB),
        name="token",
    )(slot_row, arrived.reshape(2 * total, width // 2))


def solution(mesh):
    token_spec = P(AXES, None)
    weight_spec = P(AXES, None, None)
    return jax.shard_map(
        per_device,
        mesh=mesh,
        in_specs=(token_spec, token_spec, P(AXES), P(AXES), weight_spec, weight_spec),
        out_specs=token_spec,
        check_vma=False,
    )
```

```python
import functools

import jax
import jax.numpy as jnp
from jax import lax
from jax.experimental import pallas as pl
from jax.experimental.pallas import tpu as pltpu
from jax.sharding import PartitionSpec as P

CAP = 2
AXES = ("cross", "island")
MIB = 1 << 20
TILE = 256
UNITS = 2
PRE, BACK, FINAL = range(3)


def ramp(pre):
    return jnp.clip(0.5 + 10.0 * pre, 0.0, 1.0)


def split(value, size):
    if size & (size - 1) == 0:
        return value >> (size.bit_length() - 1), value & (size - 1)
    return lax.div(value, size), lax.rem(value, size)


def one_hot(mask):
    return jnp.where(mask, 1.0, 0.0).astype(jnp.bfloat16)


def start_kernel(out_ref):
    out_ref[...] = jnp.zeros_like(out_ref)


def send_kernel(
    per_dev, slot_ref, gate_ref, tokens_ref, cotangent_ref, started, out_ref
):
    del started
    shape = (out_ref.shape[0], slot_ref.shape[1])
    device, within = split(lax.broadcasted_iota(jnp.int32, shape, 0), 2 * per_dev)
    kind, place = split(within, per_dev)
    match = slot_ref[...] == device * per_dev + place
    is_d = kind == 1
    rows = jnp.dot(
        one_hot(match & ~is_d), tokens_ref[...], preferred_element_type=jnp.float32
    ) + jnp.dot(
        one_hot(match & is_d), cotangent_ref[...], preferred_element_type=jnp.float32
    )
    gate = jnp.sum(jnp.where(match, gate_ref[...], 0.0), axis=1, keepdims=True)
    out_ref[...] = (rows * jnp.where(is_d[:, :1], gate, 1.0)).astype(out_ref.dtype)


def expert_kernel(experts, chunk, recv_ref, w_in_ref, w_out_ref, out_ref):
    per_dev = experts * CAP
    total = recv_ref.shape[0]
    devices = total // (2 * per_dev)
    rows = devices * CAP
    width = recv_ref.shape[1]
    hidden = w_in_ref.shape[2]
    to = lax.broadcasted_iota(jnp.int32, (total, total), 0)
    group, member = split(to, rows)
    device, cap = split(member, CAP)
    source = device * (2 * per_dev) + group * CAP + cap
    pick = one_hot(lax.broadcasted_iota(jnp.int32, (total, total), 1) == source)
    sorted_rows = jnp.dot(
        pick, recv_ref[...], preferred_element_type=jnp.float32
    ).astype(jnp.bfloat16)
    parts = []
    for e in range(experts):
        x = sorted_rows[e * rows : (e + 1) * rows]
        d = sorted_rows[(experts + e) * rows : (experts + e + 1) * rows]
        total_grad = jnp.zeros((rows, width), jnp.float32)
        for f in range(0, hidden, chunk):
            first = w_in_ref[e, :, f : f + chunk]
            second = w_out_ref[e, f : f + chunk, :]
            pre = jnp.dot(x, first, preferred_element_type=jnp.float32)
            back = lax.dot_general(
                d, second, (((1,), (1,)), ((), ())), preferred_element_type=jnp.float32
            )
            hidden_grad = (back * ramp(pre)).astype(jnp.bfloat16)
            total_grad += lax.dot_general(
                hidden_grad,
                first,
                (((1,), (1,)), ((), ())),
                preferred_element_type=jnp.float32,
            )
        parts.append(total_grad.astype(jnp.bfloat16))
    grads = jnp.concatenate(parts, axis=0)
    half = width // 2
    shape = (total, experts * rows)
    device, within = split(lax.broadcasted_iota(jnp.int32, shape, 0), 2 * per_dev)
    side, place = split(within, per_dev)
    expert, cap = split(place, CAP)
    match = lax.broadcasted_iota(jnp.int32, shape, 1) == (
        expert * rows + device * CAP + cap
    )
    out_ref[...] = (
        jnp.dot(
            one_hot(match & (side == 0)),
            grads[:, :half],
            preferred_element_type=jnp.float32,
        )
        + jnp.dot(
            one_hot(match & (side == 1)),
            grads[:, half:],
            preferred_element_type=jnp.float32,
        )
    ).astype(out_ref.dtype)


def expert_tiles_kernel(recv_ref, w_in_ref, w_out_ref, out_ref):
    experts, width, hidden = w_in_ref.shape
    per_dev = experts * CAP
    total = recv_ref.shape[0]
    devices = total // (2 * per_dev)
    rows = devices * CAP
    half = width // 2
    depth = width // TILE
    bf16 = jnp.bfloat16
    square = (total, total)

    def cut(k):
        return slice(k * TILE, (k + 1) * TILE)

    def sort_rows(*accs):
        group, member = split(lax.broadcasted_iota(jnp.int32, square, 0), rows)
        device, cap = split(member, CAP)
        source = device * (2 * per_dev) + group * CAP + cap
        pick = one_hot(lax.broadcasted_iota(jnp.int32, square, 1) == source)
        for k in range(depth):
            pltpu.matmul_push_rhs(recv_ref[:, cut(k)], k // UNITS % 2, k % UNITS)
        for k in range(depth):
            pltpu.matmul_acc_lhs(accs[k], pick, k // UNITS % 2)
        return [pltpu.matmul_pop(acc).astype(bf16) for acc in accs]

    columns = pl.run_scoped(
        sort_rows,
        *[pltpu.ACC(k % UNITS)((total, TILE), jnp.float32) for k in range(depth)],
    )

    def products(*accs):
        def acc(unit, kind, turn):
            return accs[unit * 5 + 2 * kind + turn % 2]

        plans = []
        for unit in range(UNITS):
            blocks = [
                (e, f)
                for e in range(experts)
                for f in range(unit * TILE, hidden, UNITS * TILE)
            ]
            plan = []
            for turn, (e, f) in enumerate(blocks):
                tiles = [
                    (kind, turn, e, slice(f, f + TILE), k)
                    for kind in (PRE, BACK)
                    for k in range(depth)
                ]
                if turn:
                    tiles.insert(depth + 1, final)
                plan += tiles
                final = (FINAL, turn, e, slice(f, f + TILE), 0)
            plans.append(plan + [final])
        last = len(plans[0]) - 1

        def push(unit, n):
            kind, turn, e, f, k = plans[unit][n]
            if kind == PRE:
                tile = w_in_ref[e, cut(k), f]
            elif kind == BACK:
                tile = w_out_ref[e, f, cut(k)]
            else:
                pre = pltpu.matmul_pop(acc(unit, PRE, turn))
                back = pltpu.matmul_pop(acc(unit, BACK, turn))
                parts = [(back * ramp(pre)).astype(bf16)]
                if e:
                    parts.insert(0, jnp.zeros((e * rows, TILE), bf16))
                parts.append(jnp.zeros((TILE - (e + 1) * rows, TILE), bf16))
                tile = jnp.concatenate(parts, 0)
            pltpu.matmul_push_rhs(tile, n % 2, unit, transpose=kind != PRE)

        def multiply(unit, n):
            kind, turn, e, f, k = plans[unit][n]
            if kind == FINAL:
                pltpu.matmul_acc_lhs(accs[unit * 5 + 4], w_in_ref[e, :, f], n % 2)
            else:
                group = kind * experts + e
                pltpu.matmul_acc_lhs(
                    acc(unit, kind, turn),
                    columns[k][group * rows : (group + 1) * rows],
                    n % 2,
                )

        for n in range(2):
            for unit in range(UNITS):
                push(unit, n)
        for n in range(last + 1):
            for unit in range(UNITS):
                multiply(unit, n)
                if n + 2 < last:
                    push(unit, n + 2)
                if n + 1 == last:
                    push(unit, last)
        sums = [pltpu.matmul_pop(accs[u * 5 + 4])[:, : experts * rows] for u in range(UNITS)]
        return (sums[0] + sums[1]).astype(bf16)

    spaces = []
    for unit in range(UNITS):
        spaces += [pltpu.ACC(unit)((rows, TILE), jnp.float32)] * 4
        spaces += [pltpu.ACC(unit)((width, TILE), jnp.float32)]
    grads = pl.run_scoped(products, *spaces)

    def spread(*accs):
        device, within = split(lax.broadcasted_iota(jnp.int32, square, 0), 2 * per_dev)
        side, place = split(within, per_dev)
        expert, cap = split(place, CAP)
        source = (side * experts + expert) * rows + device * CAP + cap
        put = one_hot(lax.broadcasted_iota(jnp.int32, square, 1) == source)
        sizes = [min(TILE, half - j * TILE) for j in range(len(accs))]
        for j, n in enumerate(sizes):
            tile = jnp.concatenate(
                [grads[s + j * TILE : s + j * TILE + n] for s in (0, half)], 1
            )
            if n < TILE:
                tile = jnp.concatenate([tile, jnp.zeros((TILE - n, TILE), bf16)], 0)
            pltpu.matmul_push_rhs(tile, j // UNITS, j % UNITS, transpose=True)
        for j, acc in enumerate(accs):
            pltpu.matmul_acc_lhs(acc, put, j // UNITS)
        for j, n in enumerate(sizes):
            out_ref[:, j * TILE : j * TILE + n] = pltpu.matmul_pop(accs[j])[
                :, :n
            ].astype(out_ref.dtype)

    pl.run_scoped(
        spread,
        *[
            pltpu.ACC(j % UNITS)((total, TILE), jnp.float32)
            for j in range(pl.cdiv(half, TILE))
        ],
    )


def tiles_fit(devices, experts, width, hidden):
    rows = devices * CAP
    return (
        2 * experts * rows == TILE
        and rows % 16 == 0
        and width == 3 * TILE
        and hidden % (UNITS * TILE) == 0
    )


def token_kernel(per_dev, slot_ref, rows_ref, out_ref):
    shape = (rows_ref.shape[0], slot_ref.shape[1])
    device, within = split(lax.broadcasted_iota(jnp.int32, shape, 0), 2 * per_dev)
    side, place = split(within, per_dev)
    match = slot_ref[...] == device * per_dev + place
    half = rows_ref.shape[1]
    for k in range(2):
        out_ref[:, k * half : (k + 1) * half] = lax.dot_general(
            one_hot(match & (side == k)),
            rows_ref[...],
            (((0,), (0,)), ((), ())),
            preferred_element_type=jnp.float32,
        ).astype(out_ref.dtype)


VMEM = pl.BlockSpec(memory_space=pltpu.VMEM)
LONG = pl.CostEstimate(flops=20_000_000_000, transcendentals=0, bytes_accessed=0)


def per_device(tokens, cotangent, gate, slot, w_in, w_out):
    devices = lax.axis_size("cross") * lax.axis_size("island")
    experts, width, hidden = w_in.shape
    per_dev = experts * CAP
    total = devices * per_dev
    slot_row = slot[None, :]
    started = pl.pallas_call(
        start_kernel,
        out_shape=jax.ShapeDtypeStruct((8, 128), jnp.float32),
        out_specs=VMEM,
        compiler_params=pltpu.CompilerParams(vmem_limit_bytes=MIB),
        cost_estimate=LONG,
        name="start",
    )()
    send = pl.pallas_call(
        functools.partial(send_kernel, per_dev),
        out_shape=jax.ShapeDtypeStruct((2 * total, width), jnp.bfloat16),
        in_specs=[VMEM] * 4 + [pl.BlockSpec(memory_space=pl.ANY)],
        out_specs=VMEM,
        compiler_params=pltpu.CompilerParams(vmem_limit_bytes=16 * MIB),
        cost_estimate=LONG,
        name="send",
    )(slot_row, gate[None, :], tokens, cotangent, started)
    recv = lax.all_to_all(
        send.reshape(devices, 2 * per_dev, width), AXES, 0, 0, tiled=True
    )
    result = pl.pallas_call(
        expert_tiles_kernel
        if tiles_fit(devices, experts, width, hidden)
        else functools.partial(expert_kernel, experts, 512),
        out_shape=jax.ShapeDtypeStruct((2 * total, width // 2), jnp.bfloat16),
        in_specs=[VMEM] * 3,
        out_specs=VMEM,
        compiler_params=pltpu.CompilerParams(vmem_limit_bytes=32 * MIB),
        name="expert",
    )(recv.reshape(2 * total, width), w_in, w_out)
    arrived = lax.all_to_all(
        result.reshape(devices, 2 * per_dev, width // 2), AXES, 0, 0, tiled=True
    )
    return pl.pallas_call(
        functools.partial(token_kernel, per_dev),
        out_shape=jax.ShapeDtypeStruct(tokens.shape, jnp.bfloat16),
        in_specs=[VMEM] * 2,
        out_specs=VMEM,
        compiler_params=pltpu.CompilerParams(vmem_limit_bytes=16 * MIB),
        name="token",
    )(slot_row, arrived.reshape(2 * total, width // 2))


def solution(mesh):
    token_spec = P(AXES, None)
    weight_spec = P(AXES, None, None)
    return jax.shard_map(
        per_device,
        mesh=mesh,
        in_specs=(token_spec, token_spec, P(AXES), P(AXES), weight_spec, weight_spec),
        out_specs=token_spec,
        check_vma=False,
    )
```

```python
import functools

import jax
import jax.numpy as jnp
import numpy as np
from jax import lax
from jax.experimental import pallas as pl
from jax.experimental.pallas import tpu as pltpu
from jax.sharding import PartitionSpec as P

CAP = 2
AXES = ("cross", "island")
MIB = 1 << 20
TILE = 256
UNITS = 2
CHUNK = 128
PRE, BACK, FINAL = range(3)


def ramp(pre):
    return jnp.clip(0.5 + 10.0 * pre, 0.0, 1.0)


def split(value, size):
    if size & (size - 1) == 0:
        return value >> (size.bit_length() - 1), value & (size - 1)
    return lax.div(value, size), lax.rem(value, size)


def one_hot(mask):
    return jnp.where(mask, 1.0, 0.0).astype(jnp.bfloat16)


def start_kernel(out_ref):
    out_ref[...] = jnp.zeros_like(out_ref)


def send_kernel(
    per_dev, slot_ref, gate_ref, tokens_ref, cotangent_ref, started, out_ref
):
    del started
    shape = (out_ref.shape[0], slot_ref.shape[1])
    device, within = split(lax.broadcasted_iota(jnp.int32, shape, 0), 2 * per_dev)
    kind, place = split(within, per_dev)
    match = slot_ref[...] == device * per_dev + place
    is_d = kind == 1
    rows = jnp.dot(
        one_hot(match & ~is_d), tokens_ref[...], preferred_element_type=jnp.float32
    ) + jnp.dot(
        one_hot(match & is_d), cotangent_ref[...], preferred_element_type=jnp.float32
    )
    gate = jnp.sum(jnp.where(match, gate_ref[...], 0.0), axis=1, keepdims=True)
    out_ref[...] = (rows * jnp.where(is_d[:, :1], gate, 1.0)).astype(out_ref.dtype)


def expert_kernel(experts, chunk, recv_ref, w_in_ref, w_out_ref, out_ref):
    per_dev = experts * CAP
    total = recv_ref.shape[0]
    devices = total // (2 * per_dev)
    rows = devices * CAP
    width = recv_ref.shape[1]
    hidden = w_in_ref.shape[2]
    to = lax.broadcasted_iota(jnp.int32, (total, total), 0)
    group, member = split(to, rows)
    device, cap = split(member, CAP)
    source = device * (2 * per_dev) + group * CAP + cap
    pick = one_hot(lax.broadcasted_iota(jnp.int32, (total, total), 1) == source)
    sorted_rows = jnp.dot(
        pick, recv_ref[...], preferred_element_type=jnp.float32
    ).astype(jnp.bfloat16)
    parts = []
    for e in range(experts):
        x = sorted_rows[e * rows : (e + 1) * rows]
        d = sorted_rows[(experts + e) * rows : (experts + e + 1) * rows]
        total_grad = jnp.zeros((rows, width), jnp.float32)
        for f in range(0, hidden, chunk):
            first = w_in_ref[e, :, f : f + chunk]
            second = w_out_ref[e, f : f + chunk, :]
            pre = jnp.dot(x, first, preferred_element_type=jnp.float32)
            back = lax.dot_general(
                d, second, (((1,), (1,)), ((), ())), preferred_element_type=jnp.float32
            )
            hidden_grad = (back * ramp(pre)).astype(jnp.bfloat16)
            total_grad += lax.dot_general(
                hidden_grad,
                first,
                (((1,), (1,)), ((), ())),
                preferred_element_type=jnp.float32,
            )
        parts.append(total_grad.astype(jnp.bfloat16))
    grads = jnp.concatenate(parts, axis=0)
    half = width // 2
    shape = (total, experts * rows)
    device, within = split(lax.broadcasted_iota(jnp.int32, shape, 0), 2 * per_dev)
    side, place = split(within, per_dev)
    expert, cap = split(place, CAP)
    match = lax.broadcasted_iota(jnp.int32, shape, 1) == (
        expert * rows + device * CAP + cap
    )
    out_ref[...] = (
        jnp.dot(
            one_hot(match & (side == 0)),
            grads[:, :half],
            preferred_element_type=jnp.float32,
        )
        + jnp.dot(
            one_hot(match & (side == 1)),
            grads[:, half:],
            preferred_element_type=jnp.float32,
        )
    ).astype(out_ref.dtype)


def expert_tiles_kernel(recv_ref, w_in_ref, w_out_ref, pick_ref, put_ref, out_ref):
    experts, width, hidden = w_in_ref.shape
    per_dev = experts * CAP
    total = recv_ref.shape[0]
    devices = total // (2 * per_dev)
    rows = devices * CAP
    half = width // 2
    depth = width // TILE
    bf16 = jnp.bfloat16

    def cut(k):
        return slice(k * TILE, (k + 1) * TILE)

    def sort_rows(*accs):
        for k in range(depth):
            pltpu.matmul_push_rhs(recv_ref[:, cut(k)], k // UNITS % 2, k % UNITS)
        for k in range(depth):
            pltpu.matmul_acc_lhs(accs[k], pick_ref[...], k // UNITS % 2)
        return [pltpu.matmul_pop(acc).astype(bf16) for acc in accs]

    columns = pl.run_scoped(
        sort_rows,
        *[pltpu.ACC(k % UNITS)((total, TILE), jnp.float32) for k in range(depth)],
    )

    def products(*accs):
        def acc(unit, kind, turn):
            return accs[unit * 5 + 2 * kind + turn % 2]

        plans = []
        for unit in range(UNITS):
            blocks = [
                (e, f)
                for e in range(experts)
                for f in range(unit * TILE, hidden, UNITS * TILE)
            ]
            plan = []
            for turn, (e, f) in enumerate(blocks):
                tiles = [
                    (kind, turn, e, slice(f, f + TILE), k)
                    for kind in (PRE, BACK)
                    for k in range(depth)
                ]
                if turn:
                    tiles.insert(depth + 1, final)
                plan += tiles
                final = (FINAL, turn, e, slice(f, f + TILE), 0)
            plans.append(plan + [final])
        last = len(plans[0]) - 1

        def push(unit, n):
            kind, turn, e, f, k = plans[unit][n]
            if kind == PRE:
                tile = w_in_ref[e, cut(k), f]
            elif kind == BACK:
                tile = w_out_ref[e, f, cut(k)]
            else:
                pre = pltpu.matmul_pop(acc(unit, PRE, turn))
                back = pltpu.matmul_pop(acc(unit, BACK, turn))
                parts = [(back * ramp(pre)).astype(bf16)]
                if e:
                    parts.insert(0, jnp.zeros((e * rows, TILE), bf16))
                parts.append(jnp.zeros((TILE - (e + 1) * rows, TILE), bf16))
                tile = jnp.concatenate(parts, 0)
            pltpu.matmul_push_rhs(tile, n % 2, unit, transpose=kind != PRE)

        def multiply(unit, n):
            kind, turn, e, f, k = plans[unit][n]
            if kind == FINAL:
                pltpu.matmul_acc_lhs(accs[unit * 5 + 4], w_in_ref[e, :, f], n % 2)
            else:
                group = kind * experts + e
                pltpu.matmul_acc_lhs(
                    acc(unit, kind, turn),
                    columns[k][group * rows : (group + 1) * rows],
                    n % 2,
                )

        for n in range(2):
            for unit in range(UNITS):
                push(unit, n)
        for n in range(last + 1):
            for unit in range(UNITS):
                multiply(unit, n)
                if n + 2 < last:
                    push(unit, n + 2)
                if n + 1 == last:
                    push(unit, last)
        sums = [pltpu.matmul_pop(accs[u * 5 + 4])[:, : experts * rows] for u in range(UNITS)]
        return (sums[0] + sums[1]).astype(bf16)

    spaces = []
    for unit in range(UNITS):
        spaces += [pltpu.ACC(unit)((rows, TILE), jnp.float32)] * 4
        spaces += [pltpu.ACC(unit)((width, TILE), jnp.float32)]
    grads = pl.run_scoped(products, *spaces)

    def spread(*accs):
        sizes = [min(TILE, half - j * TILE) for j in range(len(accs))]
        for j, n in enumerate(sizes):
            tile = jnp.concatenate(
                [grads[s + j * TILE : s + j * TILE + n] for s in (0, half)], 1
            )
            if n < TILE:
                tile = jnp.concatenate([tile, jnp.zeros((TILE - n, TILE), bf16)], 0)
            pltpu.matmul_push_rhs(tile, j // UNITS, j % UNITS, transpose=True)
        for j, acc in enumerate(accs):
            pltpu.matmul_acc_lhs(acc, put_ref[...], j // UNITS)
        for j, n in enumerate(sizes):
            out_ref[:, j * TILE : j * TILE + n] = pltpu.matmul_pop(accs[j])[
                :, :n
            ].astype(out_ref.dtype)

    pl.run_scoped(
        spread,
        *[
            pltpu.ACC(j % UNITS)((total, TILE), jnp.float32)
            for j in range(pl.cdiv(half, TILE))
        ],
    )


def row_orders(devices, experts):
    total = 2 * devices * experts * CAP
    source = (
        np.arange(total).reshape(devices, 2 * experts, CAP).transpose(1, 0, 2).ravel()
    )
    pick = (source[:, None] == np.arange(total)).astype(jnp.bfloat16)
    return pick, np.ascontiguousarray(pick.T)


def tiles_fit(devices, experts, width, hidden):
    rows = devices * CAP
    return (
        2 * experts * rows == TILE
        and rows % 16 == 0
        and width == 3 * TILE
        and hidden % (UNITS * TILE) == 0
    )


def token_kernel(per_dev, slot_ref, rows_ref, out_hbm, out_ref, sems):
    total, half = rows_ref.shape
    device, within = split(
        lax.broadcasted_iota(jnp.int32, (CHUNK, total), 1), 2 * per_dev
    )
    side, place = split(within, per_dev)
    wanted = device * per_dev + place
    copies = []
    for c in range(slot_ref.shape[1] // CHUNK):
        tokens = pl.ds(c * CHUNK, CHUNK)
        slot = jnp.broadcast_to(slot_ref[:, tokens], (CHUNK, CHUNK)).T
        slot = jnp.concatenate([slot] * (total // CHUNK), axis=1)
        for k in range(2):
            out_ref[tokens, k * half : (k + 1) * half] = jnp.dot(
                one_hot((slot == wanted) & (side == k)),
                rows_ref[...],
                preferred_element_type=jnp.float32,
            ).astype(out_ref.dtype)
        copies.append(
            pltpu.make_async_copy(out_ref.at[tokens], out_hbm.at[tokens], sems.at[c])
        )
        copies[-1].start()
    for copy in copies:
        copy.wait()


VMEM = pl.BlockSpec(memory_space=pltpu.VMEM)
SHORT = pl.CostEstimate(flops=4_000_000_000, transcendentals=0, bytes_accessed=0)
LONG = pl.CostEstimate(flops=20_000_000_000, transcendentals=0, bytes_accessed=0)


def per_device(tokens, cotangent, gate, slot, w_in, w_out):
    devices = lax.axis_size("cross") * lax.axis_size("island")
    experts, width, hidden = w_in.shape
    per_dev = experts * CAP
    total = devices * per_dev
    slot_row = slot[None, :]
    started = pl.pallas_call(
        start_kernel,
        out_shape=jax.ShapeDtypeStruct((8, 128), jnp.float32),
        out_specs=VMEM,
        compiler_params=pltpu.CompilerParams(vmem_limit_bytes=MIB),
        cost_estimate=SHORT,
        name="start",
    )()
    send = pl.pallas_call(
        functools.partial(send_kernel, per_dev),
        out_shape=jax.ShapeDtypeStruct((2 * total, width), jnp.bfloat16),
        in_specs=[VMEM] * 4 + [pl.BlockSpec(memory_space=pl.ANY)],
        out_specs=VMEM,
        compiler_params=pltpu.CompilerParams(vmem_limit_bytes=16 * MIB),
        cost_estimate=LONG,
        name="send",
    )(slot_row, gate[None, :], tokens, cotangent, started)
    recv = lax.all_to_all(
        send.reshape(devices, 2 * per_dev, width), AXES, 0, 0, tiled=True
    )
    operands = (recv.reshape(2 * total, width), w_in, w_out)
    kernel = functools.partial(expert_kernel, experts, 512)
    if tiles_fit(devices, experts, width, hidden):
        operands += tuple(jnp.asarray(m) for m in row_orders(devices, experts))
        kernel = expert_tiles_kernel
    result = pl.pallas_call(
        kernel,
        out_shape=jax.ShapeDtypeStruct((2 * total, width // 2), jnp.bfloat16),
        in_specs=[VMEM] * len(operands),
        out_specs=VMEM,
        compiler_params=pltpu.CompilerParams(vmem_limit_bytes=32 * MIB),
        name="expert",
    )(*operands)
    arrived = lax.all_to_all(
        result.reshape(devices, 2 * per_dev, width // 2), AXES, 0, 0, tiled=True
    )
    return pl.pallas_call(
        functools.partial(token_kernel, per_dev),
        out_shape=jax.ShapeDtypeStruct(tokens.shape, jnp.bfloat16),
        in_specs=[VMEM] * 2,
        out_specs=pl.BlockSpec(memory_space=pl.ANY),
        scratch_shapes=[
            pltpu.VMEM(tokens.shape, tokens.dtype),
            pltpu.SemaphoreType.DMA((tokens.shape[0] // CHUNK,)),
        ],
        compiler_params=pltpu.CompilerParams(vmem_limit_bytes=16 * MIB),
        name="token",
    )(slot_row, arrived.reshape(2 * total, width // 2))


def solution(mesh):
    token_spec = P(AXES, None)
    weight_spec = P(AXES, None, None)
    return jax.shard_map(
        per_device,
        mesh=mesh,
        in_specs=(token_spec, token_spec, P(AXES), P(AXES), weight_spec, weight_spec),
        out_specs=token_spec,
        check_vma=False,
    )
```

```python
import functools

import jax
import jax.numpy as jnp
import numpy as np
from jax import lax
from jax.experimental import pallas as pl
from jax.experimental.pallas import tpu as pltpu
from jax.sharding import PartitionSpec as P

CAP = 2
AXES = ("cross", "island")
MIB = 1 << 20
TILE = 256
UNITS = 2
CHUNK = 128
PRE, BACK, FINAL = range(3)


def ramp(pre):
    return jnp.clip(0.5 + 10.0 * pre, 0.0, 1.0)


def split(value, size):
    if size & (size - 1) == 0:
        return value >> (size.bit_length() - 1), value & (size - 1)
    return lax.div(value, size), lax.rem(value, size)


def one_hot(mask):
    return jnp.where(mask, 1.0, 0.0).astype(jnp.bfloat16)


def send_kernel(per_dev, *refs):
    sources, (out_ref, done_ref, *held, sems) = refs[:4], refs[4:]
    copies = [
        pltpu.make_async_copy(source, ref, sems.at[i])
        for i, (source, ref) in enumerate(zip(sources, held))
    ]
    for copy in copies:
        copy.start()
    slot_ref, gate_ref, tokens_ref, cotangent_ref = held
    shape = (out_ref.shape[0], slot_ref.shape[1])
    device, within = split(lax.broadcasted_iota(jnp.int32, shape, 0), 2 * per_dev)
    kind, place = split(within, per_dev)
    is_d = kind == 1
    copies[0].wait()
    match = slot_ref[...] == device * per_dev + place
    pick_x, pick_d = one_hot(match & ~is_d), one_hot(match & is_d)
    copies[1].wait()
    gate = jnp.sum(jnp.where(match, gate_ref[...], 0.0), axis=1, keepdims=True)
    scale = jnp.where(is_d[:, :1], gate, 1.0)
    copies[2].wait()
    rows = jnp.dot(pick_x, tokens_ref[...], preferred_element_type=jnp.float32)
    copies[3].wait()
    rows += jnp.dot(pick_d, cotangent_ref[...], preferred_element_type=jnp.float32)
    out_ref[...] = (rows * scale).astype(out_ref.dtype)
    done_ref[...] = jnp.zeros_like(done_ref)


def fetch_kernel(done_ref, out_ref):
    del done_ref
    out_ref[...] = jnp.zeros_like(out_ref)


def expert_kernel(experts, chunk, _, recv_ref, w_in_ref, w_out_ref, out_ref):
    per_dev = experts * CAP
    total = recv_ref.shape[0]
    devices = total // (2 * per_dev)
    rows = devices * CAP
    width = recv_ref.shape[1]
    hidden = w_in_ref.shape[2]
    to = lax.broadcasted_iota(jnp.int32, (total, total), 0)
    group, member = split(to, rows)
    device, cap = split(member, CAP)
    source = device * (2 * per_dev) + group * CAP + cap
    pick = one_hot(lax.broadcasted_iota(jnp.int32, (total, total), 1) == source)
    sorted_rows = jnp.dot(
        pick, recv_ref[...], preferred_element_type=jnp.float32
    ).astype(jnp.bfloat16)
    parts = []
    for e in range(experts):
        x = sorted_rows[e * rows : (e + 1) * rows]
        d = sorted_rows[(experts + e) * rows : (experts + e + 1) * rows]
        total_grad = jnp.zeros((rows, width), jnp.float32)
        for f in range(0, hidden, chunk):
            first = w_in_ref[e, :, f : f + chunk]
            second = w_out_ref[e, f : f + chunk, :]
            pre = jnp.dot(x, first, preferred_element_type=jnp.float32)
            back = lax.dot_general(
                d, second, (((1,), (1,)), ((), ())), preferred_element_type=jnp.float32
            )
            hidden_grad = (back * ramp(pre)).astype(jnp.bfloat16)
            total_grad += lax.dot_general(
                hidden_grad,
                first,
                (((1,), (1,)), ((), ())),
                preferred_element_type=jnp.float32,
            )
        parts.append(total_grad.astype(jnp.bfloat16))
    grads = jnp.concatenate(parts, axis=0)
    half = width // 2
    shape = (total, experts * rows)
    device, within = split(lax.broadcasted_iota(jnp.int32, shape, 0), 2 * per_dev)
    side, place = split(within, per_dev)
    expert, cap = split(place, CAP)
    match = lax.broadcasted_iota(jnp.int32, shape, 1) == (
        expert * rows + device * CAP + cap
    )
    out_ref[...] = (
        jnp.dot(
            one_hot(match & (side == 0)),
            grads[:, :half],
            preferred_element_type=jnp.float32,
        )
        + jnp.dot(
            one_hot(match & (side == 1)),
            grads[:, half:],
            preferred_element_type=jnp.float32,
        )
    ).astype(out_ref.dtype)


def expert_tiles_kernel(_, recv_ref, w_in_ref, w_out_ref, pick_ref, put_ref, out_ref):
    experts, width, hidden = w_in_ref.shape
    per_dev = experts * CAP
    total = recv_ref.shape[0]
    devices = total // (2 * per_dev)
    rows = devices * CAP
    half = width // 2
    depth = width // TILE
    bf16 = jnp.bfloat16

    def cut(k):
        return slice(k * TILE, (k + 1) * TILE)

    def sort_rows(*accs):
        for k in range(depth):
            pltpu.matmul_push_rhs(recv_ref[:, cut(k)], k // UNITS % 2, k % UNITS)
        for k in range(depth):
            pltpu.matmul_acc_lhs(accs[k], pick_ref[...], k // UNITS % 2)
        return [pltpu.matmul_pop(acc).astype(bf16) for acc in accs]

    columns = pl.run_scoped(
        sort_rows,
        *[pltpu.ACC(k % UNITS)((total, TILE), jnp.float32) for k in range(depth)],
    )

    def products(*accs):
        def acc(unit, kind, turn):
            return accs[unit * 5 + 2 * kind + turn % 2]

        plans = []
        for unit in range(UNITS):
            blocks = [
                (e, f)
                for e in range(experts)
                for f in range(unit * TILE, hidden, UNITS * TILE)
            ]
            plan = []
            for turn, (e, f) in enumerate(blocks):
                tiles = [
                    (kind, turn, e, slice(f, f + TILE), k)
                    for kind in (PRE, BACK)
                    for k in range(depth)
                ]
                if turn:
                    tiles.insert(depth + 1, final)
                plan += tiles
                final = (FINAL, turn, e, slice(f, f + TILE), 0)
            plans.append(plan + [final])
        last = len(plans[0]) - 1

        def push(unit, n):
            kind, turn, e, f, k = plans[unit][n]
            if kind == PRE:
                tile = w_in_ref[e, cut(k), f]
            elif kind == BACK:
                tile = w_out_ref[e, f, cut(k)]
            else:
                pre = pltpu.matmul_pop(acc(unit, PRE, turn))
                back = pltpu.matmul_pop(acc(unit, BACK, turn))
                parts = [(back * ramp(pre)).astype(bf16)]
                if e:
                    parts.insert(0, jnp.zeros((e * rows, TILE), bf16))
                parts.append(jnp.zeros((TILE - (e + 1) * rows, TILE), bf16))
                tile = jnp.concatenate(parts, 0)
            pltpu.matmul_push_rhs(tile, n % 2, unit, transpose=kind != PRE)

        def multiply(unit, n):
            kind, turn, e, f, k = plans[unit][n]
            if kind == FINAL:
                pltpu.matmul_acc_lhs(accs[unit * 5 + 4], w_in_ref[e, :, f], n % 2)
            else:
                group = kind * experts + e
                pltpu.matmul_acc_lhs(
                    acc(unit, kind, turn),
                    columns[k][group * rows : (group + 1) * rows],
                    n % 2,
                )

        for n in range(2):
            for unit in range(UNITS):
                push(unit, n)
        for n in range(last + 1):
            for unit in range(UNITS):
                multiply(unit, n)
                if n + 2 < last:
                    push(unit, n + 2)
                if n + 1 == last:
                    push(unit, last)
        sums = [pltpu.matmul_pop(accs[u * 5 + 4])[:, : experts * rows] for u in range(UNITS)]
        return (sums[0] + sums[1]).astype(bf16)

    spaces = []
    for unit in range(UNITS):
        spaces += [pltpu.ACC(unit)((rows, TILE), jnp.float32)] * 4
        spaces += [pltpu.ACC(unit)((width, TILE), jnp.float32)]
    grads = pl.run_scoped(products, *spaces)

    def spread(*accs):
        sizes = [min(TILE, half - j * TILE) for j in range(len(accs))]
        for j, n in enumerate(sizes):
            tile = jnp.concatenate(
                [grads[s + j * TILE : s + j * TILE + n] for s in (0, half)], 1
            )
            if n < TILE:
                tile = jnp.concatenate([tile, jnp.zeros((TILE - n, TILE), bf16)], 0)
            pltpu.matmul_push_rhs(tile, j // UNITS, j % UNITS, transpose=True)
        for j, acc in enumerate(accs):
            pltpu.matmul_acc_lhs(acc, put_ref[...], j // UNITS)
        for j, n in enumerate(sizes):
            out_ref[:, j * TILE : j * TILE + n] = pltpu.matmul_pop(accs[j])[
                :, :n
            ].astype(out_ref.dtype)

    pl.run_scoped(
        spread,
        *[
            pltpu.ACC(j % UNITS)((total, TILE), jnp.float32)
            for j in range(pl.cdiv(half, TILE))
        ],
    )


def row_orders(devices, experts):
    total = 2 * devices * experts * CAP
    source = (
        np.arange(total).reshape(devices, 2 * experts, CAP).transpose(1, 0, 2).ravel()
    )
    pick = (source[:, None] == np.arange(total)).astype(jnp.bfloat16)
    return pick, np.ascontiguousarray(pick.T)


def tiles_fit(devices, experts, width, hidden):
    rows = devices * CAP
    return (
        2 * experts * rows == TILE
        and rows % 16 == 0
        and width == 3 * TILE
        and hidden % (UNITS * TILE) == 0
    )


def token_kernel(per_dev, slot_ref, rows_ref, out_hbm, out_ref, sems):
    total, half = rows_ref.shape
    device, within = split(
        lax.broadcasted_iota(jnp.int32, (CHUNK, total), 1), 2 * per_dev
    )
    side, place = split(within, per_dev)
    wanted = device * per_dev + place
    copies = []
    for c in range(slot_ref.shape[1] // CHUNK):
        tokens = pl.ds(c * CHUNK, CHUNK)
        slot = jnp.broadcast_to(slot_ref[:, tokens], (CHUNK, CHUNK)).T
        slot = jnp.concatenate([slot] * (total // CHUNK), axis=1)
        for k in range(2):
            out_ref[tokens, k * half : (k + 1) * half] = jnp.dot(
                one_hot((slot == wanted) & (side == k)),
                rows_ref[...],
                preferred_element_type=jnp.float32,
            ).astype(out_ref.dtype)
        copies.append(
            pltpu.make_async_copy(out_ref.at[tokens], out_hbm.at[tokens], sems.at[c])
        )
        copies[-1].start()
    for copy in copies:
        copy.wait()


VMEM = pl.BlockSpec(memory_space=pltpu.VMEM)
ANY = pl.BlockSpec(memory_space=pl.ANY)
LONG = pl.CostEstimate(flops=20_000_000_000, transcendentals=0, bytes_accessed=0)


def per_device(tokens, cotangent, gate, slot, w_in, w_out):
    devices = lax.axis_size("cross") * lax.axis_size("island")
    experts, width, hidden = w_in.shape
    per_dev = experts * CAP
    total = devices * per_dev
    slot_row = slot[None, :]
    arrays = (slot_row, gate[None, :], tokens, cotangent)
    arrays = [pltpu.with_memory_space_constraint(a, pltpu.HBM) for a in arrays]
    mark = jax.ShapeDtypeStruct((8, 128), jnp.float32)
    send, sent = pl.pallas_call(
        functools.partial(send_kernel, per_dev),
        out_shape=(jax.ShapeDtypeStruct((2 * total, width), jnp.bfloat16), mark),
        in_specs=[ANY] * 4,
        out_specs=(VMEM, VMEM),
        scratch_shapes=[pltpu.VMEM(a.shape, a.dtype) for a in arrays]
        + [pltpu.SemaphoreType.DMA((4,))],
        compiler_params=pltpu.CompilerParams(vmem_limit_bytes=16 * MIB),
        name="send",
    )(*arrays)
    fetch = pl.pallas_call(
        fetch_kernel,
        out_shape=mark,
        in_specs=[ANY],
        out_specs=VMEM,
        compiler_params=pltpu.CompilerParams(vmem_limit_bytes=MIB),
        cost_estimate=LONG,
        name="fetch",
    )(sent)
    send, fetch = lax.optimization_barrier((send, fetch))
    recv = lax.all_to_all(
        send.reshape(devices, 2 * per_dev, width), AXES, 0, 0, tiled=True
    )
    operands = (fetch, recv.reshape(2 * total, width), w_in, w_out)
    kernel = functools.partial(expert_kernel, experts, 512)
    if tiles_fit(devices, experts, width, hidden):
        operands += tuple(jnp.asarray(m) for m in row_orders(devices, experts))
        kernel = expert_tiles_kernel
    result = pl.pallas_call(
        kernel,
        out_shape=jax.ShapeDtypeStruct((2 * total, width // 2), jnp.bfloat16),
        in_specs=[ANY] + [VMEM] * (len(operands) - 1),
        out_specs=VMEM,
        compiler_params=pltpu.CompilerParams(vmem_limit_bytes=32 * MIB),
        name="expert",
    )(*operands)
    arrived = lax.all_to_all(
        result.reshape(devices, 2 * per_dev, width // 2), AXES, 0, 0, tiled=True
    )
    return pl.pallas_call(
        functools.partial(token_kernel, per_dev),
        out_shape=jax.ShapeDtypeStruct(tokens.shape, jnp.bfloat16),
        in_specs=[VMEM] * 2,
        out_specs=ANY,
        scratch_shapes=[
            pltpu.VMEM(tokens.shape, tokens.dtype),
            pltpu.SemaphoreType.DMA((tokens.shape[0] // CHUNK,)),
        ],
        compiler_params=pltpu.CompilerParams(vmem_limit_bytes=16 * MIB),
        name="token",
    )(slot_row, arrived.reshape(2 * total, width // 2))


def solution(mesh):
    token_spec = P(AXES, None)
    weight_spec = P(AXES, None, None)
    return jax.shard_map(
        per_device,
        mesh=mesh,
        in_specs=(token_spec, token_spec, P(AXES), P(AXES), weight_spec, weight_spec),
        out_specs=token_spec,
        check_vma=False,
    )
```

```python
import functools

import jax
import jax.numpy as jnp
import numpy as np
from jax import lax
from jax.experimental import pallas as pl
from jax.experimental.pallas import tpu as pltpu
from jax.sharding import PartitionSpec as P

CAP = 2
AXES = ("cross", "island")
MIB = 1 << 20
TILE = 256
UNITS = 2
CHUNK = 128
PRE, BACK, FINAL = range(3)


def ramp(pre):
    return jnp.clip(0.5 + 10.0 * pre, 0.0, 1.0)


def split(value, size):
    if size & (size - 1) == 0:
        return value >> (size.bit_length() - 1), value & (size - 1)
    return lax.div(value, size), lax.rem(value, size)


def one_hot(mask):
    return jnp.where(mask, 1.0, 0.0).astype(jnp.bfloat16)


def start_kernel(out_ref):
    out_ref[...] = jnp.zeros_like(out_ref)


def plan_kernel(per_dev, slot_ref, gate_ref, _, x_ref, d_ref, scale_ref, back_ref):
    shape = x_ref.shape
    device, within = split(lax.broadcasted_iota(jnp.int32, shape, 0), 2 * per_dev)
    kind, place = split(within, per_dev)
    match = slot_ref[...] == device * per_dev + place
    is_d = kind == 1
    x_ref[...] = one_hot(match & ~is_d)
    d_ref[...] = one_hot(match & is_d)
    gate = jnp.sum(jnp.where(match, gate_ref[...], 0.0), axis=1, keepdims=True)
    scale = jnp.where(is_d[:, :1], gate, 1.0)
    scale_ref[...] = jnp.broadcast_to(scale, scale_ref.shape)
    _, count, total = back_ref.shape
    device, within = split(
        lax.broadcasted_iota(jnp.int32, (CHUNK, total), 1), 2 * per_dev
    )
    side, place = split(within, per_dev)
    wanted = device * per_dev + place
    for c in range(0, count, CHUNK):
        slot = jnp.broadcast_to(slot_ref[:, c : c + CHUNK], (CHUNK, CHUNK)).T
        slot = jnp.concatenate([slot] * (total // CHUNK), axis=1)
        for k in range(2):
            back_ref[k, c : c + CHUNK] = one_hot((slot == wanted) & (side == k))


def send_kernel(x_ref, d_ref, scale_ref, tokens_ref, cotangent_ref, out_ref):
    rows = jnp.dot(x_ref[...], tokens_ref[...], preferred_element_type=jnp.float32)
    rows += jnp.dot(d_ref[...], cotangent_ref[...], preferred_element_type=jnp.float32)
    out_ref[...] = (rows * scale_ref[:, :1]).astype(out_ref.dtype)


def expert_kernel(experts, chunk, recv_ref, w_in_ref, w_out_ref, out_ref):
    per_dev = experts * CAP
    total = recv_ref.shape[0]
    devices = total // (2 * per_dev)
    rows = devices * CAP
    width = recv_ref.shape[1]
    hidden = w_in_ref.shape[2]
    to = lax.broadcasted_iota(jnp.int32, (total, total), 0)
    group, member = split(to, rows)
    device, cap = split(member, CAP)
    source = device * (2 * per_dev) + group * CAP + cap
    pick = one_hot(lax.broadcasted_iota(jnp.int32, (total, total), 1) == source)
    sorted_rows = jnp.dot(
        pick, recv_ref[...], preferred_element_type=jnp.float32
    ).astype(jnp.bfloat16)
    parts = []
    for e in range(experts):
        x = sorted_rows[e * rows : (e + 1) * rows]
        d = sorted_rows[(experts + e) * rows : (experts + e + 1) * rows]
        total_grad = jnp.zeros((rows, width), jnp.float32)
        for f in range(0, hidden, chunk):
            first = w_in_ref[e, :, f : f + chunk]
            second = w_out_ref[e, f : f + chunk, :]
            pre = jnp.dot(x, first, preferred_element_type=jnp.float32)
            back = lax.dot_general(
                d, second, (((1,), (1,)), ((), ())), preferred_element_type=jnp.float32
            )
            hidden_grad = (back * ramp(pre)).astype(jnp.bfloat16)
            total_grad += lax.dot_general(
                hidden_grad,
                first,
                (((1,), (1,)), ((), ())),
                preferred_element_type=jnp.float32,
            )
        parts.append(total_grad.astype(jnp.bfloat16))
    grads = jnp.concatenate(parts, axis=0)
    half = width // 2
    shape = (total, experts * rows)
    device, within = split(lax.broadcasted_iota(jnp.int32, shape, 0), 2 * per_dev)
    side, place = split(within, per_dev)
    expert, cap = split(place, CAP)
    match = lax.broadcasted_iota(jnp.int32, shape, 1) == (
        expert * rows + device * CAP + cap
    )
    out_ref[...] = (
        jnp.dot(
            one_hot(match & (side == 0)),
            grads[:, :half],
            preferred_element_type=jnp.float32,
        )
        + jnp.dot(
            one_hot(match & (side == 1)),
            grads[:, half:],
            preferred_element_type=jnp.float32,
        )
    ).astype(out_ref.dtype)


def expert_tiles_kernel(recv_ref, w_in_ref, w_out_ref, pick_ref, put_ref, out_ref):
    experts, width, hidden = w_in_ref.shape
    per_dev = experts * CAP
    total = recv_ref.shape[0]
    devices = total // (2 * per_dev)
    rows = devices * CAP
    half = width // 2
    depth = width // TILE
    bf16 = jnp.bfloat16

    def cut(k):
        return slice(k * TILE, (k + 1) * TILE)

    def sort_rows(*accs):
        for k in range(depth):
            pltpu.matmul_push_rhs(recv_ref[:, cut(k)], k // UNITS % 2, k % UNITS)
        for k in range(depth):
            pltpu.matmul_acc_lhs(accs[k], pick_ref[...], k // UNITS % 2)
        return [pltpu.matmul_pop(acc).astype(bf16) for acc in accs]

    columns = pl.run_scoped(
        sort_rows,
        *[pltpu.ACC(k % UNITS)((total, TILE), jnp.float32) for k in range(depth)],
    )

    def products(*accs):
        def acc(unit, kind, turn):
            return accs[unit * 5 + 2 * kind + turn % 2]

        plans = []
        for unit in range(UNITS):
            blocks = [
                (e, f)
                for e in range(experts)
                for f in range(unit * TILE, hidden, UNITS * TILE)
            ]
            plan = []
            for turn, (e, f) in enumerate(blocks):
                plan += [
                    (kind, turn, e, slice(f, f + TILE), k)
                    for kind in (BACK, PRE)
                    for k in range(depth)
                ]
                if turn:
                    plan.append(final)
                final = (FINAL, turn, e, slice(f, f + TILE), 0)
            plans.append(plan + [final])
        last = len(plans[0]) - 1

        def push(unit, n):
            kind, turn, e, f, k = plans[unit][n]
            if kind == PRE:
                tile = w_in_ref[e, cut(k), f]
            elif kind == BACK:
                tile = w_out_ref[e, f, cut(k)]
            else:
                pre = pltpu.matmul_pop(acc(unit, PRE, turn))
                back = pltpu.matmul_pop(acc(unit, BACK, turn))
                parts = [jnp.zeros((rows, TILE), bf16)] * experts
                parts[e] = (back * ramp(pre)).astype(bf16)
                tile = jnp.concatenate(parts, 0).T
                rest = jnp.zeros((TILE, TILE - experts * rows), bf16)
                tile = jnp.concatenate([tile, rest], 1)
            pltpu.matmul_push_rhs(tile, n % 2, unit, transpose=kind == BACK)

        def multiply(unit, n):
            kind, turn, e, f, k = plans[unit][n]
            if kind == FINAL:
                pltpu.matmul_acc_lhs(accs[unit * 5 + 4], w_in_ref[e, :, f], n % 2)
            else:
                group = kind * experts + e
                pltpu.matmul_acc_lhs(
                    acc(unit, kind, turn),
                    columns[k][group * rows : (group + 1) * rows],
                    n % 2,
                )

        for n in range(2):
            for unit in range(UNITS):
                push(unit, n)
        for n in range(last + 1):
            for unit in range(UNITS):
                multiply(unit, n)
                if n + 2 < last:
                    push(unit, n + 2)
                if n + 1 == last:
                    push(unit, last)
        sums = [pltpu.matmul_pop(accs[u * 5 + 4])[:, : experts * rows] for u in range(UNITS)]
        return (sums[0] + sums[1]).astype(bf16)

    spaces = []
    for unit in range(UNITS):
        spaces += [pltpu.ACC(unit)((rows, TILE), jnp.float32)] * 4
        spaces += [pltpu.ACC(unit)((width, TILE), jnp.float32)]
    grads = pl.run_scoped(products, *spaces)

    def spread(*accs):
        sizes = [min(TILE, half - j * TILE) for j in range(len(accs))]
        for j, n in enumerate(sizes):
            tile = jnp.concatenate(
                [grads[s + j * TILE : s + j * TILE + n] for s in (0, half)], 1
            )
            if n < TILE:
                tile = jnp.concatenate([tile, jnp.zeros((TILE - n, TILE), bf16)], 0)
            pltpu.matmul_push_rhs(tile, j // UNITS, j % UNITS, transpose=True)
        for j, acc in enumerate(accs):
            pltpu.matmul_acc_lhs(acc, put_ref[...], j // UNITS)
        for j, n in enumerate(sizes):
            out_ref[:, j * TILE : j * TILE + n] = pltpu.matmul_pop(accs[j])[
                :, :n
            ].astype(out_ref.dtype)

    pl.run_scoped(
        spread,
        *[
            pltpu.ACC(j % UNITS)((total, TILE), jnp.float32)
            for j in range(pl.cdiv(half, TILE))
        ],
    )


def row_orders(devices, experts):
    total = 2 * devices * experts * CAP
    source = (
        np.arange(total).reshape(devices, 2 * experts, CAP).transpose(1, 0, 2).ravel()
    )
    pick = (source[:, None] == np.arange(total)).astype(jnp.bfloat16)
    return pick, np.ascontiguousarray(pick.T)


def tiles_fit(devices, experts, width, hidden):
    rows = devices * CAP
    return (
        2 * experts * rows == TILE
        and rows % 16 == 0
        and width == 3 * TILE
        and hidden % (UNITS * TILE) == 0
    )


def token_kernel(back_ref, rows_ref, out_hbm, out_ref, sems):
    half = rows_ref.shape[1]
    copies = []
    for c in range(out_ref.shape[0] // CHUNK):
        tokens = pl.ds(c * CHUNK, CHUNK)
        for k in range(2):
            out_ref[tokens, k * half : (k + 1) * half] = jnp.dot(
                back_ref[k, tokens],
                rows_ref[...],
                preferred_element_type=jnp.float32,
            ).astype(out_ref.dtype)
        copies.append(
            pltpu.make_async_copy(out_ref.at[tokens], out_hbm.at[tokens], sems.at[c])
        )
        copies[-1].start()
    for copy in copies:
        copy.wait()


VMEM = pl.BlockSpec(memory_space=pltpu.VMEM)
SHORT = pl.CostEstimate(flops=4_000_000_000, transcendentals=0, bytes_accessed=0)
LONG = pl.CostEstimate(flops=20_000_000_000, transcendentals=0, bytes_accessed=0)


def per_device(tokens, cotangent, gate, slot, w_in, w_out):
    devices = lax.axis_size("cross") * lax.axis_size("island")
    experts, width, hidden = w_in.shape
    per_dev = experts * CAP
    total = devices * per_dev
    slot_row = slot[None, :]
    started = pl.pallas_call(
        start_kernel,
        out_shape=jax.ShapeDtypeStruct((8, 128), jnp.float32),
        out_specs=VMEM,
        compiler_params=pltpu.CompilerParams(vmem_limit_bytes=MIB),
        cost_estimate=SHORT,
        name="start",
    )()
    picks = jax.ShapeDtypeStruct((2 * total, tokens.shape[0]), jnp.bfloat16)
    *plan, back = pl.pallas_call(
        functools.partial(plan_kernel, per_dev),
        out_shape=(
            picks,
            picks,
            jax.ShapeDtypeStruct((2 * total, 128), jnp.float32),
            jax.ShapeDtypeStruct((2, tokens.shape[0], 2 * total), jnp.bfloat16),
        ),
        in_specs=[VMEM, VMEM, pl.BlockSpec(memory_space=pl.ANY)],
        out_specs=(VMEM,) * 4,
        compiler_params=pltpu.CompilerParams(vmem_limit_bytes=16 * MIB),
        name="plan",
    )(slot_row, gate[None, :], started)
    send = pl.pallas_call(
        send_kernel,
        out_shape=jax.ShapeDtypeStruct((2 * total, width), jnp.bfloat16),
        in_specs=[VMEM] * 5,
        out_specs=VMEM,
        compiler_params=pltpu.CompilerParams(vmem_limit_bytes=16 * MIB),
        cost_estimate=LONG,
        name="send",
    )(*plan, tokens, cotangent)
    recv = lax.all_to_all(
        send.reshape(devices, 2 * per_dev, width), AXES, 0, 0, tiled=True
    )
    operands = (recv.reshape(2 * total, width), w_in, w_out)
    kernel = functools.partial(expert_kernel, experts, 512)
    if tiles_fit(devices, experts, width, hidden):
        operands += tuple(jnp.asarray(m) for m in row_orders(devices, experts))
        kernel = expert_tiles_kernel
    result = pl.pallas_call(
        kernel,
        out_shape=jax.ShapeDtypeStruct((2 * total, width // 2), jnp.bfloat16),
        in_specs=[VMEM] * len(operands),
        out_specs=VMEM,
        compiler_params=pltpu.CompilerParams(vmem_limit_bytes=32 * MIB),
        name="expert",
    )(*operands)
    arrived = lax.all_to_all(
        result.reshape(devices, 2 * per_dev, width // 2), AXES, 0, 0, tiled=True
    )
    return pl.pallas_call(
        token_kernel,
        out_shape=jax.ShapeDtypeStruct(tokens.shape, jnp.bfloat16),
        in_specs=[VMEM] * 2,
        out_specs=pl.BlockSpec(memory_space=pl.ANY),
        scratch_shapes=[
            pltpu.VMEM(tokens.shape, tokens.dtype),
            pltpu.SemaphoreType.DMA((tokens.shape[0] // CHUNK,)),
        ],
        compiler_params=pltpu.CompilerParams(vmem_limit_bytes=16 * MIB),
        name="token",
    )(back, arrived.reshape(2 * total, width // 2))


def solution(mesh):
    token_spec = P(AXES, None)
    weight_spec = P(AXES, None, None)
    return jax.shard_map(
        per_device,
        mesh=mesh,
        in_specs=(token_spec, token_spec, P(AXES), P(AXES), weight_spec, weight_spec),
        out_specs=token_spec,
        check_vma=False,
    )
```

```python
import functools

import jax
import jax.numpy as jnp
import numpy as np
from jax import lax
from jax.experimental import pallas as pl
from jax.experimental.pallas import tpu as pltpu
from jax.sharding import PartitionSpec as P

CAP = 2
AXES = ("cross", "island")
MIB = 1 << 20
TILE = 256
UNITS = 2
CHUNK = 128
PRE, BACK, FINAL = range(3)


def ramp(pre):
    return jnp.clip(0.5 + 10.0 * pre, 0.0, 1.0)


def split(value, size):
    if size & (size - 1) == 0:
        return value >> (size.bit_length() - 1), value & (size - 1)
    return lax.div(value, size), lax.rem(value, size)


def one_hot(mask):
    return jnp.where(mask, 1.0, 0.0).astype(jnp.bfloat16)


def start_kernel(out_ref):
    out_ref[...] = jnp.zeros_like(out_ref)


def plan_kernel(per_dev, slot_ref, gate_ref, _, x_ref, d_ref, scale_ref, back_ref):
    shape = x_ref.shape
    device, within = split(lax.broadcasted_iota(jnp.int32, shape, 0), 2 * per_dev)
    kind, place = split(within, per_dev)
    match = slot_ref[...] == device * per_dev + place
    is_d = kind == 1
    x_ref[...] = one_hot(match & ~is_d)
    d_ref[...] = one_hot(match & is_d)
    gate = jnp.sum(jnp.where(match, gate_ref[...], 0.0), axis=1, keepdims=True)
    scale = jnp.where(is_d[:, :1], gate, 1.0)
    scale_ref[...] = jnp.broadcast_to(scale, scale_ref.shape)
    _, count, total = back_ref.shape
    device, within = split(
        lax.broadcasted_iota(jnp.int32, (CHUNK, total), 1), 2 * per_dev
    )
    side, place = split(within, per_dev)
    wanted = device * per_dev + place
    for c in range(0, count, CHUNK):
        slot = jnp.broadcast_to(slot_ref[:, c : c + CHUNK], (CHUNK, CHUNK)).T
        slot = jnp.concatenate([slot] * (total // CHUNK), axis=1)
        for k in range(2):
            back_ref[k, c : c + CHUNK] = one_hot((slot == wanted) & (side == k))


def tokens_kernel(x_ref, tokens_ref, out_ref):
    out_ref[...] = jnp.dot(
        x_ref[...], tokens_ref[...], preferred_element_type=jnp.float32
    ).astype(out_ref.dtype)


def send_kernel(rows_ref, d_ref, scale_ref, cotangent_ref, out_ref):
    rows = jnp.dot(d_ref[...], cotangent_ref[...], preferred_element_type=jnp.float32)
    rows = rows * scale_ref[:, :1] + rows_ref[...].astype(jnp.float32)
    out_ref[...] = rows.astype(out_ref.dtype)


def expert_kernel(experts, chunk, recv_ref, w_in_ref, w_out_ref, out_ref):
    per_dev = experts * CAP
    total = recv_ref.shape[0]
    devices = total // (2 * per_dev)
    rows = devices * CAP
    width = recv_ref.shape[1]
    hidden = w_in_ref.shape[2]
    to = lax.broadcasted_iota(jnp.int32, (total, total), 0)
    group, member = split(to, rows)
    device, cap = split(member, CAP)
    source = device * (2 * per_dev) + group * CAP + cap
    pick = one_hot(lax.broadcasted_iota(jnp.int32, (total, total), 1) == source)
    sorted_rows = jnp.dot(
        pick, recv_ref[...], preferred_element_type=jnp.float32
    ).astype(jnp.bfloat16)
    parts = []
    for e in range(experts):
        x = sorted_rows[e * rows : (e + 1) * rows]
        d = sorted_rows[(experts + e) * rows : (experts + e + 1) * rows]
        total_grad = jnp.zeros((rows, width), jnp.float32)
        for f in range(0, hidden, chunk):
            first = w_in_ref[e, :, f : f + chunk]
            second = w_out_ref[e, f : f + chunk, :]
            pre = jnp.dot(x, first, preferred_element_type=jnp.float32)
            back = lax.dot_general(
                d, second, (((1,), (1,)), ((), ())), preferred_element_type=jnp.float32
            )
            hidden_grad = (back * ramp(pre)).astype(jnp.bfloat16)
            total_grad += lax.dot_general(
                hidden_grad,
                first,
                (((1,), (1,)), ((), ())),
                preferred_element_type=jnp.float32,
            )
        parts.append(total_grad.astype(jnp.bfloat16))
    grads = jnp.concatenate(parts, axis=0)
    half = width // 2
    shape = (total, experts * rows)
    device, within = split(lax.broadcasted_iota(jnp.int32, shape, 0), 2 * per_dev)
    side, place = split(within, per_dev)
    expert, cap = split(place, CAP)
    match = lax.broadcasted_iota(jnp.int32, shape, 1) == (
        expert * rows + device * CAP + cap
    )
    out_ref[...] = (
        jnp.dot(
            one_hot(match & (side == 0)),
            grads[:, :half],
            preferred_element_type=jnp.float32,
        )
        + jnp.dot(
            one_hot(match & (side == 1)),
            grads[:, half:],
            preferred_element_type=jnp.float32,
        )
    ).astype(out_ref.dtype)


def expert_tiles_kernel(recv_ref, w_in_ref, w_out_ref, pick_ref, put_ref, out_ref):
    experts, width, hidden = w_in_ref.shape
    per_dev = experts * CAP
    total = recv_ref.shape[0]
    devices = total // (2 * per_dev)
    rows = devices * CAP
    half = width // 2
    depth = width // TILE
    bf16 = jnp.bfloat16

    def cut(k):
        return slice(k * TILE, (k + 1) * TILE)

    def sort_rows(*accs):
        for k in range(depth):
            pltpu.matmul_push_rhs(recv_ref[:, cut(k)], k // UNITS % 2, k % UNITS)
        for k in range(depth):
            pltpu.matmul_acc_lhs(accs[k], pick_ref[...], k // UNITS % 2)
        return [pltpu.matmul_pop(acc).astype(bf16) for acc in accs]

    columns = pl.run_scoped(
        sort_rows,
        *[pltpu.ACC(k % UNITS)((total, TILE), jnp.float32) for k in range(depth)],
    )

    def products(*accs):
        def acc(unit, kind, turn):
            return accs[unit * 5 + 2 * kind + turn % 2]

        plans = []
        for unit in range(UNITS):
            blocks = [
                (e, f)
                for e in range(experts)
                for f in range(unit * TILE, hidden, UNITS * TILE)
            ]
            plan = []
            for turn, (e, f) in enumerate(blocks):
                plan += [
                    (kind, turn, e, slice(f, f + TILE), k)
                    for kind in (BACK, PRE)
                    for k in range(depth)
                ]
                if turn:
                    plan.append(final)
                final = (FINAL, turn, e, slice(f, f + TILE), 0)
            plans.append(plan + [final])
        last = len(plans[0]) - 1

        def push(unit, n):
            kind, turn, e, f, k = plans[unit][n]
            if kind == PRE:
                tile = w_in_ref[e, cut(k), f]
            elif kind == BACK:
                tile = w_out_ref[e, f, cut(k)]
            else:
                pre = pltpu.matmul_pop(acc(unit, PRE, turn))
                back = pltpu.matmul_pop(acc(unit, BACK, turn))
                parts = [jnp.zeros((rows, TILE), bf16)] * experts
                parts[e] = (back * ramp(pre)).astype(bf16)
                tile = jnp.concatenate(parts, 0).T
                rest = jnp.zeros((TILE, TILE - experts * rows), bf16)
                tile = jnp.concatenate([tile, rest], 1)
            pltpu.matmul_push_rhs(tile, n % 2, unit, transpose=kind == BACK)

        def multiply(unit, n):
            kind, turn, e, f, k = plans[unit][n]
            if kind == FINAL:
                pltpu.matmul_acc_lhs(accs[unit * 5 + 4], w_in_ref[e, :, f], n % 2)
            else:
                group = kind * experts + e
                pltpu.matmul_acc_lhs(
                    acc(unit, kind, turn),
                    columns[k][group * rows : (group + 1) * rows],
                    n % 2,
                )

        for n in range(2):
            for unit in range(UNITS):
                push(unit, n)
        for n in range(last + 1):
            for unit in range(UNITS):
                multiply(unit, n)
                if n + 2 < last:
                    push(unit, n + 2)
                if n + 1 == last:
                    push(unit, last)
        sums = [pltpu.matmul_pop(accs[u * 5 + 4])[:, : experts * rows] for u in range(UNITS)]
        return (sums[0] + sums[1]).astype(bf16)

    spaces = []
    for unit in range(UNITS):
        spaces += [pltpu.ACC(unit)((rows, TILE), jnp.float32)] * 4
        spaces += [pltpu.ACC(unit)((width, TILE), jnp.float32)]
    grads = pl.run_scoped(products, *spaces)

    def spread(*accs):
        sizes = [min(TILE, half - j * TILE) for j in range(len(accs))]
        for j, n in enumerate(sizes):
            tile = jnp.concatenate(
                [grads[s + j * TILE : s + j * TILE + n] for s in (0, half)], 1
            )
            if n < TILE:
                tile = jnp.concatenate([tile, jnp.zeros((TILE - n, TILE), bf16)], 0)
            pltpu.matmul_push_rhs(tile, j // UNITS, j % UNITS, transpose=True)
        for j, acc in enumerate(accs):
            pltpu.matmul_acc_lhs(acc, put_ref[...], j // UNITS)
        for j, n in enumerate(sizes):
            out_ref[:, j * TILE : j * TILE + n] = pltpu.matmul_pop(accs[j])[
                :, :n
            ].astype(out_ref.dtype)

    pl.run_scoped(
        spread,
        *[
            pltpu.ACC(j % UNITS)((total, TILE), jnp.float32)
            for j in range(pl.cdiv(half, TILE))
        ],
    )


def row_orders(devices, experts):
    total = 2 * devices * experts * CAP
    source = (
        np.arange(total).reshape(devices, 2 * experts, CAP).transpose(1, 0, 2).ravel()
    )
    pick = (source[:, None] == np.arange(total)).astype(jnp.bfloat16)
    return pick, np.ascontiguousarray(pick.T)


def tiles_fit(devices, experts, width, hidden):
    rows = devices * CAP
    return (
        2 * experts * rows == TILE
        and rows % 16 == 0
        and width == 3 * TILE
        and hidden % (UNITS * TILE) == 0
    )


def token_kernel(back_ref, rows_ref, out_hbm, out_ref, sems):
    half = rows_ref.shape[1]
    copies = []
    for c in range(out_ref.shape[0] // CHUNK):
        tokens = pl.ds(c * CHUNK, CHUNK)
        for k in range(2):
            out_ref[tokens, k * half : (k + 1) * half] = jnp.dot(
                back_ref[k, tokens],
                rows_ref[...],
                preferred_element_type=jnp.float32,
            ).astype(out_ref.dtype)
        copies.append(
            pltpu.make_async_copy(out_ref.at[tokens], out_hbm.at[tokens], sems.at[c])
        )
        copies[-1].start()
    for copy in copies:
        copy.wait()


VMEM = pl.BlockSpec(memory_space=pltpu.VMEM)
SHORT = pl.CostEstimate(flops=4_000_000_000, transcendentals=0, bytes_accessed=0)
LONG = pl.CostEstimate(flops=20_000_000_000, transcendentals=0, bytes_accessed=0)


def per_device(tokens, cotangent, gate, slot, w_in, w_out):
    devices = lax.axis_size("cross") * lax.axis_size("island")
    experts, width, hidden = w_in.shape
    per_dev = experts * CAP
    total = devices * per_dev
    slot_row = slot[None, :]
    started = pl.pallas_call(
        start_kernel,
        out_shape=jax.ShapeDtypeStruct((8, 128), jnp.float32),
        out_specs=VMEM,
        compiler_params=pltpu.CompilerParams(vmem_limit_bytes=MIB),
        cost_estimate=SHORT,
        name="start",
    )()
    picks = jax.ShapeDtypeStruct((2 * total, tokens.shape[0]), jnp.bfloat16)
    *plan, back = pl.pallas_call(
        functools.partial(plan_kernel, per_dev),
        out_shape=(
            picks,
            picks,
            jax.ShapeDtypeStruct((2 * total, 128), jnp.float32),
            jax.ShapeDtypeStruct((2, tokens.shape[0], 2 * total), jnp.bfloat16),
        ),
        in_specs=[VMEM, VMEM, pl.BlockSpec(memory_space=pl.ANY)],
        out_specs=(VMEM,) * 4,
        compiler_params=pltpu.CompilerParams(vmem_limit_bytes=16 * MIB),
        name="plan",
    )(slot_row, gate[None, :], started)
    pick_x, pick_d, scale = plan
    rows = jax.ShapeDtypeStruct((2 * total, width), jnp.bfloat16)
    placed = pl.pallas_call(
        tokens_kernel,
        out_shape=rows,
        in_specs=[VMEM] * 2,
        out_specs=VMEM,
        compiler_params=pltpu.CompilerParams(vmem_limit_bytes=16 * MIB),
        name="tokens",
    )(pick_x, tokens)
    send = pl.pallas_call(
        send_kernel,
        out_shape=rows,
        in_specs=[VMEM] * 4,
        out_specs=VMEM,
        compiler_params=pltpu.CompilerParams(vmem_limit_bytes=16 * MIB),
        cost_estimate=LONG,
        name="send",
    )(placed, pick_d, scale, cotangent)
    recv = lax.all_to_all(
        send.reshape(devices, 2 * per_dev, width), AXES, 0, 0, tiled=True
    )
    operands = (recv.reshape(2 * total, width), w_in, w_out)
    kernel = functools.partial(expert_kernel, experts, 512)
    if tiles_fit(devices, experts, width, hidden):
        operands += tuple(jnp.asarray(m) for m in row_orders(devices, experts))
        kernel = expert_tiles_kernel
    result = pl.pallas_call(
        kernel,
        out_shape=jax.ShapeDtypeStruct((2 * total, width // 2), jnp.bfloat16),
        in_specs=[VMEM] * len(operands),
        out_specs=VMEM,
        compiler_params=pltpu.CompilerParams(vmem_limit_bytes=32 * MIB),
        name="expert",
    )(*operands)
    arrived = lax.all_to_all(
        result.reshape(devices, 2 * per_dev, width // 2), AXES, 0, 0, tiled=True
    )
    return pl.pallas_call(
        token_kernel,
        out_shape=jax.ShapeDtypeStruct(tokens.shape, jnp.bfloat16),
        in_specs=[VMEM] * 2,
        out_specs=pl.BlockSpec(memory_space=pl.ANY),
        scratch_shapes=[
            pltpu.VMEM(tokens.shape, tokens.dtype),
            pltpu.SemaphoreType.DMA((tokens.shape[0] // CHUNK,)),
        ],
        compiler_params=pltpu.CompilerParams(vmem_limit_bytes=16 * MIB),
        name="token",
    )(back, arrived.reshape(2 * total, width // 2))


def solution(mesh):
    token_spec = P(AXES, None)
    weight_spec = P(AXES, None, None)
    return jax.shard_map(
        per_device,
        mesh=mesh,
        in_specs=(token_spec, token_spec, P(AXES), P(AXES), weight_spec, weight_spec),
        out_specs=token_spec,
        check_vma=False,
    )
```

```python
import functools

import jax
import jax.numpy as jnp
import numpy as np
from jax import lax
from jax.experimental import pallas as pl
from jax.experimental.pallas import tpu as pltpu
from jax.sharding import PartitionSpec as P

CAP = 2
AXES = ("cross", "island")
MIB = 1 << 20
TILE = 256
UNITS = 2
CHUNK = 128
LEAVE = 256
PRE, BACK, FINAL = range(3)


def ramp(pre):
    return jnp.clip(0.5 + 10.0 * pre, 0.0, 1.0)


def split(value, size):
    if size & (size - 1) == 0:
        return value >> (size.bit_length() - 1), value & (size - 1)
    return lax.div(value, size), lax.rem(value, size)


def one_hot(mask):
    return jnp.where(mask, 1.0, 0.0).astype(jnp.bfloat16)


def start_kernel(out_ref):
    out_ref[...] = jnp.zeros_like(out_ref)


def plan_kernel(per_dev, slot_ref, gate_ref, _, x_ref, d_ref, scale_ref, back_ref):
    shape = x_ref.shape
    device, within = split(lax.broadcasted_iota(jnp.int32, shape, 0), 2 * per_dev)
    kind, place = split(within, per_dev)
    match = slot_ref[...] == device * per_dev + place
    is_d = kind == 1
    x_ref[...] = one_hot(match & ~is_d)
    d_ref[...] = one_hot(match & is_d)
    gate = jnp.sum(jnp.where(match, gate_ref[...], 0.0), axis=1, keepdims=True)
    scale = jnp.where(is_d[:, :1], gate, 1.0)
    scale_ref[...] = jnp.broadcast_to(scale, scale_ref.shape)
    _, count, total = back_ref.shape
    device, within = split(
        lax.broadcasted_iota(jnp.int32, (CHUNK, total), 1), 2 * per_dev
    )
    side, place = split(within, per_dev)
    wanted = device * per_dev + place
    for c in range(0, count, CHUNK):
        slot = jnp.broadcast_to(slot_ref[:, c : c + CHUNK], (CHUNK, CHUNK)).T
        slot = jnp.concatenate([slot] * (total // CHUNK), axis=1)
        for k in range(2):
            back_ref[k, c : c + CHUNK] = one_hot((slot == wanted) & (side == k))


def send_kernel(x_ref, d_ref, scale_ref, tokens_ref, cotangent_ref, out_ref):
    rows = jnp.dot(x_ref[...], tokens_ref[...], preferred_element_type=jnp.float32)
    rows += jnp.dot(d_ref[...], cotangent_ref[...], preferred_element_type=jnp.float32)
    out_ref[...] = (rows * scale_ref[:, :1]).astype(out_ref.dtype)


def expert_kernel(experts, chunk, recv_ref, w_in_ref, w_out_ref, out_ref):
    per_dev = experts * CAP
    total = recv_ref.shape[0]
    devices = total // (2 * per_dev)
    rows = devices * CAP
    width = recv_ref.shape[1]
    hidden = w_in_ref.shape[2]
    to = lax.broadcasted_iota(jnp.int32, (total, total), 0)
    group, member = split(to, rows)
    device, cap = split(member, CAP)
    source = device * (2 * per_dev) + group * CAP + cap
    pick = one_hot(lax.broadcasted_iota(jnp.int32, (total, total), 1) == source)
    sorted_rows = jnp.dot(
        pick, recv_ref[...], preferred_element_type=jnp.float32
    ).astype(jnp.bfloat16)
    parts = []
    for e in range(experts):
        x = sorted_rows[e * rows : (e + 1) * rows]
        d = sorted_rows[(experts + e) * rows : (experts + e + 1) * rows]
        total_grad = jnp.zeros((rows, width), jnp.float32)
        for f in range(0, hidden, chunk):
            first = w_in_ref[e, :, f : f + chunk]
            second = w_out_ref[e, f : f + chunk, :]
            pre = jnp.dot(x, first, preferred_element_type=jnp.float32)
            back = lax.dot_general(
                d, second, (((1,), (1,)), ((), ())), preferred_element_type=jnp.float32
            )
            hidden_grad = (back * ramp(pre)).astype(jnp.bfloat16)
            total_grad += lax.dot_general(
                hidden_grad,
                first,
                (((1,), (1,)), ((), ())),
                preferred_element_type=jnp.float32,
            )
        parts.append(total_grad.astype(jnp.bfloat16))
    grads = jnp.concatenate(parts, axis=0)
    half = width // 2
    shape = (total, experts * rows)
    device, within = split(lax.broadcasted_iota(jnp.int32, shape, 0), 2 * per_dev)
    side, place = split(within, per_dev)
    expert, cap = split(place, CAP)
    match = lax.broadcasted_iota(jnp.int32, shape, 1) == (
        expert * rows + device * CAP + cap
    )
    out_ref[...] = (
        jnp.dot(
            one_hot(match & (side == 0)),
            grads[:, :half],
            preferred_element_type=jnp.float32,
        )
        + jnp.dot(
            one_hot(match & (side == 1)),
            grads[:, half:],
            preferred_element_type=jnp.float32,
        )
    ).astype(out_ref.dtype)


def expert_tiles_kernel(recv_ref, w_in_ref, w_out_ref, pick_ref, put_ref, out_ref):
    experts, width, hidden = w_in_ref.shape
    per_dev = experts * CAP
    total = recv_ref.shape[0]
    devices = total // (2 * per_dev)
    rows = devices * CAP
    half = width // 2
    depth = width // TILE
    bf16 = jnp.bfloat16

    def cut(k):
        return slice(k * TILE, (k + 1) * TILE)

    def sort_rows(*accs):
        for k in range(depth):
            pltpu.matmul_push_rhs(recv_ref[:, cut(k)], k // UNITS % 2, k % UNITS)
        for k in range(depth):
            pltpu.matmul_acc_lhs(accs[k], pick_ref[...], k // UNITS % 2)
        return [pltpu.matmul_pop(acc).astype(bf16) for acc in accs]

    columns = pl.run_scoped(
        sort_rows,
        *[pltpu.ACC(k % UNITS)((total, TILE), jnp.float32) for k in range(depth)],
    )

    def products(*accs):
        def acc(unit, kind, turn):
            return accs[unit * 5 + 2 * kind + turn % 2]

        plans = []
        for unit in range(UNITS):
            blocks = [
                (e, f)
                for e in range(experts)
                for f in range(unit * TILE, hidden, UNITS * TILE)
            ]
            plan = []
            for turn, (e, f) in enumerate(blocks):
                plan += [
                    (kind, turn, e, slice(f, f + TILE), k)
                    for kind in (BACK, PRE)
                    for k in range(depth)
                ]
                if turn:
                    plan.append(final)
                final = (FINAL, turn, e, slice(f, f + TILE), 0)
            plans.append(plan + [final])
        last = len(plans[0]) - 1

        def push(unit, n):
            kind, turn, e, f, k = plans[unit][n]
            if kind == PRE:
                tile = w_in_ref[e, cut(k), f]
            elif kind == BACK:
                tile = w_out_ref[e, f, cut(k)]
            else:
                pre = pltpu.matmul_pop(acc(unit, PRE, turn))
                back = pltpu.matmul_pop(acc(unit, BACK, turn))
                parts = [jnp.zeros((rows, TILE), bf16)] * experts
                parts[e] = (back * ramp(pre)).astype(bf16)
                tile = jnp.concatenate(parts, 0).T
                rest = jnp.zeros((TILE, TILE - experts * rows), bf16)
                tile = jnp.concatenate([tile, rest], 1)
            pltpu.matmul_push_rhs(tile, n % 2, unit, transpose=kind == BACK)

        def multiply(unit, n):
            kind, turn, e, f, k = plans[unit][n]
            if kind == FINAL:
                pltpu.matmul_acc_lhs(accs[unit * 5 + 4], w_in_ref[e, :, f], n % 2)
            else:
                group = kind * experts + e
                pltpu.matmul_acc_lhs(
                    acc(unit, kind, turn),
                    columns[k][group * rows : (group + 1) * rows],
                    n % 2,
                )

        for n in range(2):
            for unit in range(UNITS):
                push(unit, n)
        for n in range(last + 1):
            for unit in range(UNITS):
                multiply(unit, n)
                if n + 2 < last:
                    push(unit, n + 2)
                if n + 1 == last:
                    push(unit, last)
        sums = [pltpu.matmul_pop(accs[u * 5 + 4])[:, : experts * rows] for u in range(UNITS)]
        return (sums[0] + sums[1]).astype(bf16)

    spaces = []
    for unit in range(UNITS):
        spaces += [pltpu.ACC(unit)((rows, TILE), jnp.float32)] * 4
        spaces += [pltpu.ACC(unit)((width, TILE), jnp.float32)]
    grads = pl.run_scoped(products, *spaces)

    def spread(*accs):
        sizes = [min(TILE, half - j * TILE) for j in range(len(accs))]
        for j, n in enumerate(sizes):
            tile = jnp.concatenate(
                [grads[s + j * TILE : s + j * TILE + n] for s in (0, half)], 1
            )
            if n < TILE:
                tile = jnp.concatenate([tile, jnp.zeros((TILE - n, TILE), bf16)], 0)
            pltpu.matmul_push_rhs(tile, j // UNITS, j % UNITS, transpose=True)
        for j, acc in enumerate(accs):
            pltpu.matmul_acc_lhs(acc, put_ref[...], j // UNITS)
        for j, n in enumerate(sizes):
            out_ref[:, j * TILE : j * TILE + n] = pltpu.matmul_pop(accs[j])[
                :, :n
            ].astype(out_ref.dtype)

    pl.run_scoped(
        spread,
        *[
            pltpu.ACC(j % UNITS)((total, TILE), jnp.float32)
            for j in range(pl.cdiv(half, TILE))
        ],
    )


def row_orders(devices, experts):
    total = 2 * devices * experts * CAP
    source = (
        np.arange(total).reshape(devices, 2 * experts, CAP).transpose(1, 0, 2).ravel()
    )
    pick = (source[:, None] == np.arange(total)).astype(jnp.bfloat16)
    return pick, np.ascontiguousarray(pick.T)


def tiles_fit(devices, experts, width, hidden):
    rows = devices * CAP
    return (
        2 * experts * rows == TILE
        and rows % 16 == 0
        and width == 3 * TILE
        and hidden % (UNITS * TILE) == 0
    )


def token_kernel(back_ref, rows_ref, out_hbm, out_ref, sems):
    half = rows_ref.shape[1]
    copies = []
    for c in range(out_ref.shape[0] // LEAVE):
        tokens = pl.ds(c * LEAVE, LEAVE)
        for k in range(2):
            out_ref[tokens, k * half : (k + 1) * half] = jnp.dot(
                back_ref[k, tokens],
                rows_ref[...],
                preferred_element_type=jnp.float32,
            ).astype(out_ref.dtype)
        copies.append(
            pltpu.make_async_copy(out_ref.at[tokens], out_hbm.at[tokens], sems.at[c])
        )
        copies[-1].start()
    for copy in copies:
        copy.wait()


VMEM = pl.BlockSpec(memory_space=pltpu.VMEM)
SHORT = pl.CostEstimate(flops=4_000_000_000, transcendentals=0, bytes_accessed=0)
LONG = pl.CostEstimate(flops=20_000_000_000, transcendentals=0, bytes_accessed=0)


def per_device(tokens, cotangent, gate, slot, w_in, w_out):
    devices = lax.axis_size("cross") * lax.axis_size("island")
    experts, width, hidden = w_in.shape
    per_dev = experts * CAP
    total = devices * per_dev
    slot_row = slot[None, :]
    started = pl.pallas_call(
        start_kernel,
        out_shape=jax.ShapeDtypeStruct((8, 128), jnp.float32),
        out_specs=VMEM,
        compiler_params=pltpu.CompilerParams(vmem_limit_bytes=MIB),
        cost_estimate=SHORT,
        name="start",
    )()
    picks = jax.ShapeDtypeStruct((2 * total, tokens.shape[0]), jnp.bfloat16)
    *plan, back = pl.pallas_call(
        functools.partial(plan_kernel, per_dev),
        out_shape=(
            picks,
            picks,
            jax.ShapeDtypeStruct((2 * total, 128), jnp.float32),
            jax.ShapeDtypeStruct((2, tokens.shape[0], 2 * total), jnp.bfloat16),
        ),
        in_specs=[VMEM, VMEM, pl.BlockSpec(memory_space=pl.ANY)],
        out_specs=(VMEM,) * 4,
        compiler_params=pltpu.CompilerParams(vmem_limit_bytes=16 * MIB),
        name="plan",
    )(slot_row, gate[None, :], started)
    send = pl.pallas_call(
        send_kernel,
        out_shape=jax.ShapeDtypeStruct((2 * total, width), jnp.bfloat16),
        in_specs=[VMEM] * 5,
        out_specs=VMEM,
        compiler_params=pltpu.CompilerParams(vmem_limit_bytes=16 * MIB),
        cost_estimate=LONG,
        name="send",
    )(*plan, tokens, cotangent)
    recv = lax.all_to_all(
        send.reshape(devices, 2 * per_dev, width), AXES, 0, 0, tiled=True
    )
    operands = (recv.reshape(2 * total, width), w_in, w_out)
    kernel = functools.partial(expert_kernel, experts, 512)
    if tiles_fit(devices, experts, width, hidden):
        operands += tuple(jnp.asarray(m) for m in row_orders(devices, experts))
        kernel = expert_tiles_kernel
    result = pl.pallas_call(
        kernel,
        out_shape=jax.ShapeDtypeStruct((2 * total, width // 2), jnp.bfloat16),
        in_specs=[VMEM] * len(operands),
        out_specs=VMEM,
        compiler_params=pltpu.CompilerParams(vmem_limit_bytes=32 * MIB),
        name="expert",
    )(*operands)
    arrived = lax.all_to_all(
        result.reshape(devices, 2 * per_dev, width // 2), AXES, 0, 0, tiled=True
    )
    return pl.pallas_call(
        token_kernel,
        out_shape=jax.ShapeDtypeStruct(tokens.shape, jnp.bfloat16),
        in_specs=[VMEM] * 2,
        out_specs=pl.BlockSpec(memory_space=pl.ANY),
        scratch_shapes=[
            pltpu.VMEM(tokens.shape, tokens.dtype),
            pltpu.SemaphoreType.DMA((tokens.shape[0] // LEAVE,)),
        ],
        compiler_params=pltpu.CompilerParams(vmem_limit_bytes=16 * MIB),
        name="token",
    )(back, arrived.reshape(2 * total, width // 2))


def solution(mesh):
    token_spec = P(AXES, None)
    weight_spec = P(AXES, None, None)
    return jax.shard_map(
        per_device,
        mesh=mesh,
        in_specs=(token_spec, token_spec, P(AXES), P(AXES), weight_spec, weight_spec),
        out_specs=token_spec,
        check_vma=False,
    )
```
